128 devices in a mesh: seq: 16 (over z, x), hid: 4 (over y), rep: 2 (over core).
Axes of the slice: x: 4, y: 4, z: 4, core: 2. Of those that a mesh axis runs over, the one named last changes fastest.
Arguments:
- tokens: bfloat16 [16384, 5376], P(('rep', 'seq'), 'hid'), parts along dimension 0, may hold values from -6 to 6
- norm_gain: float32 [5376], replicated, may hold values from 0.1 to 1.9
- w_query: bfloat16 [5376, 4096], P('seq', 'hid'), may hold values from -0.078125 to 0.078125
- w_key: bfloat16 [5376, 2048], P('seq', 'hid'), may hold values from -0.078125 to 0.078125
- w_value: bfloat16 [5376, 2048], P('seq', 'hid'), may hold values from -0.078125 to 0.078125
- query_gain: float32 [128], replicated, may hold values from 0.5 to 8
- key_gain: float32 [128], replicated, may hold values from 0.5 to 8
- w_out: bfloat16 [4096, 5376], P('hid', 'seq'), may hold values from -0.09375 to 0.09375
Outputs:
- attended: bfloat16 [16384, 5376], P(('rep', 'seq'), 'hid'), parts along dimension 0
The draws below stay inside these ranges and needn't reach their ends.
There are 2 independent parts, one for each index of `rep`. The reference program is written for one: setup_inputs(seed, part) draws one part's arguments, and reference() takes and returns one part's arrays. A program takes and returns all parts, laid end to end along the dimension named above; an argument that names none is the same for every part. Nothing has to cross between parts.
All inputs are finite; a program needn't handle non-finite values.
Results may differ from the reference program's by a relative error of at most 0.023.
The reference program's roundings to bfloat16 on the way (of `normed`, `qh`, `kh`, `probs`, `heads_out` and `partial_g`) count: a program that leaves them out, or rounds other values in their place, can miss the bound.
Values may be sent and summed in bfloat16 or wider, within the bound.
A program may use at most 128 MiB of HBM per device.

```python
import jax
import jax.numpy as jnp
from jax import lax

D = 5376
HEADS = 32
KEY_VALUE_HEADS = 16
HEAD_WIDTH = 128
WINDOW = 1024
QSCALE = 168
TOK_DEV = 512
DEPTH = 2
TOKENS = 8192
N_SEQ = 16
N_HID = 4


def draw_query_gain(key, part):
    inner = jax.random.fold_in(key, 11)
    return jax.random.uniform(inner, (HEAD_WIDTH,), jnp.float32, 0.5, 1.5)


def draw_key_gain(key, part):
    inner = jax.random.fold_in(key, 23)
    return jax.random.uniform(inner, (HEAD_WIDTH,), jnp.float32, 0.5, 1.5)


def steps_of(own_key, shape, pieces, least, largest):
    loudness, own = 1.0, jax.random.fold_in(own_key, 6)
    for axis_at, shards_of in pieces:
        draws = jnp.exp(jax.random.uniform(jax.random.fold_in(own, axis_at), (shards_of,), jnp.float32, least / len(pieces), largest / len(pieces)))
        loudness = loudness * jnp.repeat(draws, shape[axis_at] // shards_of).reshape([-1 if axis == axis_at else 1 for axis in range(len(shape))])
    return loudness


def bell_draw(rng, shape, spread, reach, shards=(), kind=jnp.bfloat16):
    values = spread * jax.random.normal(rng, shape, jnp.float32)
    if shards:
        values = values * steps_of(rng, shape, shards, -0.22, 0.18)
    return jnp.clip(values, -reach, reach).astype(kind)


def setup_inputs(seed: int = 0, part: int = 0) -> dict:
    key_list = jax.random.split(jax.random.key(seed), 9)
    own_keys = jax.random.split(jax.random.fold_in(key_list[8], part), 9)
    return {
        "tokens": bell_draw(own_keys[0], (TOKENS, D), 1.0, 6.0, ((0, 16), (1, 4))),
        "norm_gain": jnp.clip(1.0 + 0.18 * jax.random.normal(key_list[1], (D,), jnp.float32), 0.1, 1.9),
        "w_query": bell_draw(key_list[2], (D, HEADS * HEAD_WIDTH), D ** -0.5, 0.078125, ((0, 16), (1, 4))),
        "w_key": bell_draw(key_list[3], (D, KEY_VALUE_HEADS * HEAD_WIDTH), D ** -0.5, 0.078125, ((0, 16), (1, 4))),
        "w_value": bell_draw(key_list[4], (D, KEY_VALUE_HEADS * HEAD_WIDTH), D ** -0.5, 0.078125, ((0, 16), (1, 4))),
        "query_gain": draw_query_gain(jax.random.fold_in(key_list[8], 71), part),
        "key_gain": draw_key_gain(jax.random.fold_in(key_list[8], 71), part),
        "w_out": bell_draw(key_list[7], (HEADS * HEAD_WIDTH, D), (HEADS * HEAD_WIDTH) ** -0.5, 0.09375, ((0, 4), (1, 16))),
    }


def rope(heads, positions):
    half = heads.shape[-1] // 2
    freq = 10000.0 ** (-(jnp.arange(half, dtype=jnp.float32) * 2.0) / heads.shape[-1])
    angle = positions[:, None] * freq[None, :]
    cosine = jnp.cos(angle)[:, None, :]
    sine = jnp.sin(angle)[:, None, :]
    first = heads[..., :half]
    second = heads[..., half:]
    return jnp.concatenate([first * cosine - second * sine, second * cosine + first * sine], axis=-1)

def head_norm(heads, gain):
    return heads * lax.rsqrt(lax.optimization_barrier(jnp.mean(heads * heads, axis=-1, keepdims=True)) + 1e-06) * gain

def reference(tokens, norm_gain, w_query, w_key, w_value, query_gain, key_gain, w_out):
    xfloat = tokens.astype(jnp.float32)
    normed = (xfloat * lax.rsqrt(lax.optimization_barrier(jnp.mean(xfloat * xfloat, axis=-1, keepdims=True)) + 1e-06) * norm_gain).astype(jnp.bfloat16)
    query = jnp.dot(normed, w_query, preferred_element_type=jnp.float32).reshape(TOKENS, HEADS, HEAD_WIDTH)
    key = jnp.dot(normed, w_key, preferred_element_type=jnp.float32).reshape(TOKENS, KEY_VALUE_HEADS, HEAD_WIDTH)
    value = jnp.dot(normed, w_value, preferred_element_type=jnp.float32).reshape(TOKENS, KEY_VALUE_HEADS, HEAD_WIDTH)
    positions = jnp.arange(TOKENS).astype(jnp.float32)
    qh = (rope(head_norm(query, query_gain), positions) * QSCALE ** (-0.5)).astype(jnp.bfloat16)
    kh = rope(head_norm(key, key_gain), positions).astype(jnp.bfloat16)
    value_head = value.astype(jnp.bfloat16)
    padding_rows = DEPTH * TOK_DEV
    kpad = jnp.concatenate([jnp.zeros((padding_rows, KEY_VALUE_HEADS, HEAD_WIDTH), jnp.bfloat16), kh], axis=0)
    value_padding = jnp.concatenate([jnp.zeros((padding_rows, KEY_VALUE_HEADS, HEAD_WIDTH), jnp.bfloat16), value_head], axis=0)
    group = HEADS // KEY_VALUE_HEADS
    window_extent = (DEPTH + 1) * TOK_DEV

    def one_block(index):
        start_offset = (index * TOK_DEV).astype(jnp.int32)
        qblock = lax.dynamic_slice_in_dim(qh, start_offset, TOK_DEV, 0).reshape(TOK_DEV, KEY_VALUE_HEADS, group, HEAD_WIDTH)
        kblock = lax.dynamic_slice_in_dim(kpad, start_offset, window_extent, 0)
        value_block_rows = lax.dynamic_slice_in_dim(value_padding, start_offset, window_extent, 0)
        qpos = start_offset + jnp.arange(TOK_DEV, dtype=jnp.int32)
        kpos = start_offset - padding_rows + jnp.arange(window_extent, dtype=jnp.int32)
        diff = qpos[:, None] - kpos[None, :]
        allowed = (diff >= 0) & (diff < WINDOW) & (kpos >= 0)[None, :]
        scores = jnp.einsum('rkgd,lkd->kgrl', qblock.astype(jnp.float32), kblock.astype(jnp.float32))
        scores = jnp.where(allowed[None, None], scores, -jnp.inf)
        probs = jax.nn.softmax(scores, axis=-1).astype(jnp.bfloat16)
        mixed = jnp.einsum('kgrl,lkd->rkgd', probs.astype(jnp.float32), value_block_rows.astype(jnp.float32))
        return mixed.astype(jnp.bfloat16).reshape(TOK_DEV, HEADS * HEAD_WIDTH)
    blocks = lax.map(one_block, jnp.arange(N_SEQ, dtype=jnp.int32))
    heads_out = blocks.reshape(TOKENS, HEADS * HEAD_WIDTH)
    width = HEADS * HEAD_WIDTH // N_HID
    total = jnp.zeros((TOKENS, D), jnp.float32)
    for group_index in range(N_HID):
        lo = group_index * width
        partial_g = jnp.dot(heads_out[:, lo:lo + width], w_out[lo:lo + width], preferred_element_type=jnp.float32)
        total = total + partial_g.astype(jnp.bfloat16).astype(jnp.float32)
    return total.astype(jnp.bfloat16)
```

```python
import functools

import jax
import jax.numpy as jnp
from jax import lax
from jax.experimental import pallas as pl
from jax.experimental.pallas import tpu as pltpu
from jax.sharding import PartitionSpec as P

HEAD_WIDTH = 128
WINDOW = 1024
QSCALE = 168
DEPTH = 2
RING = 4
MESH = pl.DeviceIdType.MESH
BF16 = jnp.bfloat16
F32 = jnp.float32


def place():
    seq = lax.axis_index("seq")
    return lax.rem(seq, RING), lax.axis_index("hid"), lax.div(seq, RING), lax.axis_index("rep")


def device(x, y, z, r):
    return {"seq": z * RING + x, "hid": y, "rep": r}


def step(a, by):
    return lax.rem(a + by + RING, RING)


def send(src, dst, send_sem, recv_sem, dev):
    copy = pltpu.make_async_remote_copy(
        src_ref=src,
        dst_ref=dst,
        send_sem=send_sem,
        recv_sem=recv_sem,
        device_id=dev,
        device_id_type=MESH,
    )
    copy.start()
    return copy


def greet(devs):
    barrier = pltpu.get_barrier_semaphore()
    for dev in devs:
        pl.semaphore_signal(barrier, inc=1, device_id=dev, device_id_type=MESH)
    pl.semaphore_wait(barrier, len(devs))


def project_kernel(
    tok_ref, gain_ref, wcat_ref, qg_ref, kg_ref, cos_ref, sin_ref,
    q_ref, k_ref, v_ref,
    wbuf, xbuf, acc, sums,
    wsend, wrecv, sib_send, sib_recv, loc, ssend, srecv, xsend, xrecv,
):
    x, y, z, r = place()
    width = tok_ref.shape[0]
    rows = tok_ref.shape[1]
    one = 1 - r
    c1 = x * one + z * r
    c2 = z * one + x * r

    def along1(by):
        return device(step(x, by * one), y, step(z, by * r), r)

    def along2(by):
        return device(step(x, by * r), y, step(z, by * one), r)

    def along_y(by):
        return device(x, step(y, by), z, r)

    sibling = device(x, y, z, 1 - r)
    greet([along1(1), along1(-1), along2(1), along2(-1),
           along_y(1), along_y(-1), along_y(2), sibling])

    sent = []

    def go(*args):
        copy = send(*args)
        sent.append(copy)
        return copy

    local = []
    for ph in range(2):
        kind = 2 * ph + r
        copy = pltpu.make_async_copy(wcat_ref.at[kind], wbuf.at[kind, c2, c1], loc.at[ph])
        copy.start()
        local.append(copy)

    def stage1a(ph):
        kind = 2 * ph + r
        src, dst = wcat_ref.at[kind], wbuf.at[kind, c2, c1]
        return [go(src, dst, wsend.at[ph, i], wrecv.at[ph, i], along1(by))
                for i, by in enumerate((1, -1))]

    def stage1b(ph, before):
        kind = 2 * ph + r
        half = wbuf.shape[4] // 2
        out = []
        for i, by in enumerate((1, -1)):
            before[i].wait_recv()
            ref = wbuf.at[kind, c2, step(c1, -by), :, pl.ds(i * half, half)]
            out.append(go(ref, ref, wsend.at[ph, 2 + i], wrecv.at[ph, 2 + i], along1(by)))
        return out

    def to_sibling(ph, i, row):
        ref = wbuf.at[2 * ph + r, row]
        return go(ref, ref, sib_send.at[ph, i], sib_recv.at[ph, i], sibling)

    def stage2a(ph, before):
        kind = 2 * ph + r
        local[ph].wait()
        for copy in before:
            copy.wait_recv()
        ref = wbuf.at[kind, c2]
        out = [go(ref, ref, wsend.at[ph, 4 + i], wrecv.at[ph, 4 + i], along2(by))
               for i, by in enumerate((1, -1))]
        return out, [to_sibling(ph, 0, c2)]

    def stage2b(ph, before, sib):
        kind = 2 * ph + r
        out = []
        for i, by in enumerate((1, -1)):
            before[i].wait_recv()
            row = step(c2, -by)
            ref = wbuf.at[kind, row, pl.ds(2 * i, 2)]
            out.append(go(ref, ref, wsend.at[ph, 6 + i], wrecv.at[ph, 6 + i], along2(by)))
        for i, by in enumerate((1, -1)):
            sib.append(to_sibling(ph, 1 + i, step(c2, -by)))
        return out

    def stage2c(ph, before, sib):
        for copy in before:
            copy.wait_recv()
        sib.append(to_sibling(ph, 3, step(c2, 2)))

    a0 = stage1a(0)

    raw = tok_ref[...].astype(F32)
    sums[y] = jnp.sum(raw * raw, axis=0, keepdims=True)
    told = [go(sums.at[y], sums.at[y], ssend.at[i], srecv.at[i], along_y(by))
            for i, by in enumerate((1, 2, 3))]
    for copy in told:
        copy.wait_recv()
    total = sums[0] + sums[1] + sums[2] + sums[3]
    scale = lax.rsqrt(total * (1.0 / (RING * width)) + 1e-06)

    def norm_chunk(at, size):
        part = tok_ref[pl.ds(at, size), :].astype(F32)
        part = part * scale * gain_ref[pl.ds(at, size), :]
        xbuf[y, :, pl.ds(at, size)] = part.T.astype(BF16)

    lanes = 128

    def norm_step(i, carry):
        norm_chunk(pl.multiple_of(i * lanes, lanes), lanes)
        return carry

    lax.fori_loop(0, width // lanes, norm_step, 0)
    if width % lanes:
        norm_chunk(width // lanes * lanes, width % lanes)
    xa = [go(xbuf.at[y], xbuf.at[y], xsend.at[i], xrecv.at[i], along_y(by))
          for i, by in enumerate((1, -1))]

    b0 = stage1b(0, a0)
    d0, sib0 = stage2a(0, b0)
    a1 = stage1a(1)
    b1 = stage1b(1, a1)
    e0 = stage2b(0, d0, sib0)
    d1, sib1 = stage2a(1, b1)
    xb = []
    for i, by in enumerate((1, -1)):
        xa[i].wait_recv()
        ref = xbuf.at[step(y, -by), pl.ds(i * (rows // 2), rows // 2)]
        xb.append(go(ref, ref, xsend.at[2 + i], xrecv.at[2 + i], along_y(by)))
    stage2c(0, e0, sib0)

    def multiply(ph, h, first):
        left = xbuf[h]
        for j in range(2):
            kind = 2 * ph + j
            block = wbuf[kind, h] if j == 0 else wbuf[kind, :, h]
            part = jnp.dot(left, block.reshape(width, block.shape[2]), preferred_element_type=F32)
            if first:
                acc[kind] = part
            else:
                acc[kind] += part

    for copy in sib0:
        copy.wait_recv()
    multiply(0, y, True)
    e1 = stage2b(1, d1, sib1)
    lax.fori_loop(0, 2, lambda i, c: (multiply(0, step(y, 1 + 2 * i), False), c)[1], 0)
    for copy in xb:
        copy.wait_recv()
    multiply(0, step(y, 2), False)

    cosine, sine = cos_ref[...], sin_ref[...]

    def turn(u, gain):
        u = u * lax.rsqrt(jnp.mean(u * u, axis=-1, keepdims=True) + 1e-06) * gain
        return u * cosine + pltpu.roll(u, HEAD_WIDTH // 2, 1) * sine

    key_gain, query_gain = kg_ref[...], qg_ref[...]
    for head in range(4):
        cols = pl.ds(head * HEAD_WIDTH, HEAD_WIDTH)
        k_ref[:, cols] = turn(acc[0, :, cols], key_gain).astype(BF16)
    v_ref[...] = acc[1].astype(BF16)

    stage2c(1, e1, sib1)
    for copy in sib1:
        copy.wait_recv()
    multiply(1, y, True)
    lax.fori_loop(1, RING, lambda i, c: (multiply(1, step(y, i), False), c)[1], 0)
    for kind in range(2):
        for head in range(4):
            cols = pl.ds(head * HEAD_WIDTH, HEAD_WIDTH)
            dest = pl.ds((kind * 4 + head) * HEAD_WIDTH, HEAD_WIDTH)
            turned = turn(acc[2 + kind, :, cols], query_gain) * QSCALE ** (-0.5)
            q_ref[:, dest] = turned.astype(BF16)
    for copy in sent:
        copy.wait_send()


def project(tok, gain, wcat, query_gain, key_gain, cosine, sine):
    width, rows = tok.shape
    depth, cols = wcat.shape[1:]
    dma = pltpu.SemaphoreType.DMA
    vmem = pl.BlockSpec(memory_space=pltpu.VMEM)
    return pl.pallas_call(
        project_kernel,
        out_shape=(
            jax.ShapeDtypeStruct((rows, 2 * cols), BF16),
            jax.ShapeDtypeStruct((rows, cols), BF16),
            jax.ShapeDtypeStruct((rows, cols), BF16),
        ),
        in_specs=[vmem, vmem, pl.BlockSpec(memory_space=pl.ANY), vmem, vmem, vmem, vmem],
        out_specs=(vmem, vmem, vmem),
        scratch_shapes=[
            pltpu.VMEM((4, RING, RING, depth, cols), BF16),
            pltpu.VMEM((RING, rows, width), BF16),
            pltpu.VMEM((4, rows, cols), F32),
            pltpu.VMEM((RING, 1, rows), F32),
            dma((2, 8)), dma((2, 8)), dma((2, 4)), dma((2, 4)), dma((2,)),
            dma((3,)), dma((3,)), dma((4,)), dma((4,)),
        ],
        compiler_params=pltpu.CompilerParams(
            collective_id=0, has_side_effects=True, vmem_limit_bytes=58 * 2**20
        ),
        cost_estimate=pl.CostEstimate(
            flops=2 * rows * RING * width * 4 * cols, bytes_accessed=10**8, transcendentals=0
        ),
    )(tok, gain, wcat, query_gain, key_gain, cosine, sine)


def shifted(x, axis, by):
    count = lax.axis_size(axis)
    pairs = [(i, i + by) for i in range(count) if 0 <= i + by < count]
    return lax.ppermute(x, axis, pairs)


def shards(tokens, norm_gain, w_query, w_key, w_value, query_gain, key_gain, w_out):
    rows, width = tokens.shape
    hid = lax.axis_index("hid")
    gain = lax.dynamic_slice_in_dim(norm_gain, hid * width, width).reshape(width, 1)
    cols = w_key.shape[1]
    wcat = jnp.stack([w_key, w_value, w_query[:, :cols], w_query[:, cols:]])
    local_heads = w_query.shape[1] // HEAD_WIDTH
    local_kv = w_key.shape[1] // HEAD_WIDTH
    base = lax.axis_index("seq") * rows
    qpos = base + jnp.arange(rows, dtype=jnp.int32)
    half = HEAD_WIDTH // 2
    freq = 10000.0 ** (-(jnp.arange(half, dtype=F32) * 2.0) / HEAD_WIDTH)
    angle = qpos.astype(F32)[:, None] * freq[None, :]
    cosine, sine = jnp.cos(angle), jnp.sin(angle)
    qh, kh, value_head = project(
        tokens.T, gain, wcat,
        query_gain.reshape(1, -1), key_gain.reshape(1, -1),
        jnp.concatenate([cosine, cosine], axis=1), jnp.concatenate([-sine, sine], axis=1),
    )
    qh = qh.reshape(rows, local_heads, HEAD_WIDTH)
    kh = kh.reshape(rows, local_kv, HEAD_WIDTH)
    value_head = value_head.reshape(rows, local_kv, HEAD_WIDTH)
    key_blocks = []
    value_blocks = []
    for distance in range(1, DEPTH + 1):
        arrived = shifted((kh, value_head), "seq", distance)
        key_blocks.insert(0, arrived[0])
        value_blocks.insert(0, arrived[1])
    keys = jnp.concatenate(key_blocks + [kh], axis=0)
    values = jnp.concatenate(value_blocks + [value_head], axis=0)
    window_extent = keys.shape[0]
    kpos = base - DEPTH * rows + jnp.arange(window_extent, dtype=jnp.int32)
    diff = qpos[:, None] - kpos[None, :]
    allowed = (diff >= 0) & (diff < WINDOW) & (kpos >= 0)[None, :]
    group = local_heads // local_kv
    grouped = qh.reshape(rows, local_kv, group, HEAD_WIDTH).transpose(1, 0, 2, 3)

    def one_head(operands):
        qpart, kpart, vpart = operands
        scores = jnp.einsum("rgd,ld->grl", qpart, kpart, preferred_element_type=F32)
        scores = jnp.where(allowed[None], scores, -jnp.inf)
        probs = jax.nn.softmax(scores, axis=-1).astype(BF16)
        mixed = jnp.einsum("grl,ld->rgd", probs, vpart, preferred_element_type=F32)
        return mixed.astype(BF16)

    per_head = lax.map(one_head, (grouped, keys.transpose(1, 0, 2), values.transpose(1, 0, 2)))
    heads_out = per_head.transpose(1, 0, 2, 3).reshape(rows, local_heads * HEAD_WIDTH)
    terms = jnp.dot(
        heads_out,
        lax.all_gather(w_out, "seq", axis=1, tiled=True),
        preferred_element_type=F32,
    )
    return lax.psum_scatter(terms.astype(BF16), "hid", scatter_dimension=1, tiled=True)


def solution(mesh):
    return jax.shard_map(
        shards,
        mesh=mesh,
        in_specs=(
            P(("rep", "seq"), "hid"),
            P(),
            P("seq", "hid"),
            P("seq", "hid"),
            P("seq", "hid"),
            P(),
            P(),
            P("hid", "seq"),
        ),
        out_specs=P(("rep", "seq"), "hid"),
        check_vma=False,
    )
```

```python
import functools

import jax
import jax.numpy as jnp
from jax import lax
from jax.experimental import pallas as pl
from jax.experimental.pallas import tpu as pltpu
from jax.sharding import PartitionSpec as P

HEAD_WIDTH = 128
WINDOW = 1024
QSCALE = 168
DEPTH = 2
RING = 4
QB = 128
MESH = pl.DeviceIdType.MESH
BF16 = jnp.bfloat16
F32 = jnp.float32


def place():
    seq = lax.axis_index("seq")
    return lax.rem(seq, RING), lax.axis_index("hid"), lax.div(seq, RING), lax.axis_index("rep")


def device(x, y, z, r):
    return {"seq": z * RING + x, "hid": y, "rep": r}


def step(a, by):
    return lax.rem(a + by + RING, RING)


def send(src, dst, send_sem, recv_sem, dev):
    copy = pltpu.make_async_remote_copy(
        src_ref=src,
        dst_ref=dst,
        send_sem=send_sem,
        recv_sem=recv_sem,
        device_id=dev,
        device_id_type=MESH,
    )
    copy.start()
    return copy


def greet(devs):
    barrier = pltpu.get_barrier_semaphore()
    for dev in devs:
        pl.semaphore_signal(barrier, inc=1, device_id=dev, device_id_type=MESH)
    pl.semaphore_wait(barrier, len(devs))


def project_kernel(
    tok_ref, gain_ref, wcat_ref, qg_ref, kg_ref, cos_ref, sin_ref,
    q_ref, k_ref, v_ref,
    wbuf, xbuf, acc, sums,
    wsend, wrecv, sib_send, sib_recv, loc, ssend, srecv, xsend, xrecv,
):
    x, y, z, r = place()
    width = tok_ref.shape[0]
    rows = tok_ref.shape[1]
    one = 1 - r
    c1 = x * one + z * r
    c2 = z * one + x * r

    def along1(by):
        return device(step(x, by * one), y, step(z, by * r), r)

    def along2(by):
        return device(step(x, by * r), y, step(z, by * one), r)

    def along_y(by):
        return device(x, step(y, by), z, r)

    sibling = device(x, y, z, 1 - r)
    greet([along1(1), along1(-1), along2(1), along2(-1),
           along_y(1), along_y(-1), along_y(2), sibling])

    sent = []

    def go(*args):
        copy = send(*args)
        sent.append(copy)
        return copy

    local = []
    for ph in range(2):
        kind = 2 * ph + r
        copy = pltpu.make_async_copy(wcat_ref.at[kind], wbuf.at[kind, c2, c1], loc.at[ph])
        copy.start()
        local.append(copy)

    def stage1a(ph):
        kind = 2 * ph + r
        src, dst = wcat_ref.at[kind], wbuf.at[kind, c2, c1]
        return [go(src, dst, wsend.at[ph, i], wrecv.at[ph, i], along1(by))
                for i, by in enumerate((1, -1))]

    def stage1b(ph, before):
        kind = 2 * ph + r
        half = wbuf.shape[4] // 2
        out = []
        for i, by in enumerate((1, -1)):
            before[i].wait_recv()
            ref = wbuf.at[kind, c2, step(c1, -by), :, pl.ds(i * half, half)]
            out.append(go(ref, ref, wsend.at[ph, 2 + i], wrecv.at[ph, 2 + i], along1(by)))
        return out

    def to_sibling(ph, i, row):
        ref = wbuf.at[2 * ph + r, row]
        return go(ref, ref, sib_send.at[ph, i], sib_recv.at[ph, i], sibling)

    def stage2a(ph, before):
        kind = 2 * ph + r
        local[ph].wait()
        for copy in before:
            copy.wait_recv()
        ref = wbuf.at[kind, c2]
        out = [go(ref, ref, wsend.at[ph, 4 + i], wrecv.at[ph, 4 + i], along2(by))
               for i, by in enumerate((1, -1))]
        return out, [to_sibling(ph, 0, c2)]

    def stage2b(ph, before, sib):
        kind = 2 * ph + r
        out = []
        for i, by in enumerate((1, -1)):
            before[i].wait_recv()
            row = step(c2, -by)
            ref = wbuf.at[kind, row, pl.ds(2 * i, 2)]
            out.append(go(ref, ref, wsend.at[ph, 6 + i], wrecv.at[ph, 6 + i], along2(by)))
        for i, by in enumerate((1, -1)):
            sib.append(to_sibling(ph, 1 + i, step(c2, -by)))
        return out

    def stage2c(ph, before, sib):
        for copy in before:
            copy.wait_recv()
        sib.append(to_sibling(ph, 3, step(c2, 2)))

    a0 = stage1a(0)

    raw = tok_ref[...].astype(F32)
    sums[y] = jnp.sum(raw * raw, axis=0, keepdims=True)
    told = [go(sums.at[y], sums.at[y], ssend.at[i], srecv.at[i], along_y(by))
            for i, by in enumerate((1, 2, 3))]
    for copy in told:
        copy.wait_recv()
    total = sums[0] + sums[1] + sums[2] + sums[3]
    scale = lax.rsqrt(total * (1.0 / (RING * width)) + 1e-06)

    def norm_chunk(at, size):
        part = tok_ref[pl.ds(at, size), :].astype(F32)
        part = part * scale * gain_ref[pl.ds(at, size), :]
        xbuf[y, :, pl.ds(at, size)] = part.T.astype(BF16)

    lanes = 128

    def norm_step(i, carry):
        norm_chunk(pl.multiple_of(i * lanes, lanes), lanes)
        return carry

    lax.fori_loop(0, width // lanes, norm_step, 0)
    if width % lanes:
        norm_chunk(width // lanes * lanes, width % lanes)
    xa = [go(xbuf.at[y], xbuf.at[y], xsend.at[i], xrecv.at[i], along_y(by))
          for i, by in enumerate((1, -1))]

    b0 = stage1b(0, a0)
    d0, sib0 = stage2a(0, b0)
    a1 = stage1a(1)
    b1 = stage1b(1, a1)
    e0 = stage2b(0, d0, sib0)
    d1, sib1 = stage2a(1, b1)
    xb = []
    for i, by in enumerate((1, -1)):
        xa[i].wait_recv()
        ref = xbuf.at[step(y, -by), pl.ds(i * (rows // 2), rows // 2)]
        xb.append(go(ref, ref, xsend.at[2 + i], xrecv.at[2 + i], along_y(by)))
    stage2c(0, e0, sib0)

    def multiply(ph, h, first):
        left = xbuf[h]
        for j in range(2):
            kind = 2 * ph + j
            block = wbuf[kind, h] if j == 0 else wbuf[kind, :, h]
            part = jnp.dot(left, block.reshape(width, block.shape[2]), preferred_element_type=F32)
            if first:
                acc[kind] = part
            else:
                acc[kind] += part

    for copy in sib0:
        copy.wait_recv()
    multiply(0, y, True)
    e1 = stage2b(1, d1, sib1)
    lax.fori_loop(0, 2, lambda i, c: (multiply(0, step(y, 1 + 2 * i), False), c)[1], 0)
    for copy in xb:
        copy.wait_recv()
    multiply(0, step(y, 2), False)

    cosine, sine = cos_ref[...], sin_ref[...]

    def turn(u, gain):
        u = u * lax.rsqrt(jnp.mean(u * u, axis=-1, keepdims=True) + 1e-06) * gain
        return u * cosine + pltpu.roll(u, HEAD_WIDTH // 2, 1) * sine

    key_gain, query_gain = kg_ref[...], qg_ref[...]
    for head in range(4):
        cols = pl.ds(head * HEAD_WIDTH, HEAD_WIDTH)
        k_ref[:, cols] = turn(acc[0, :, cols], key_gain).astype(BF16)
    v_ref[...] = acc[1].astype(BF16)

    stage2c(1, e1, sib1)
    for copy in sib1:
        copy.wait_recv()
    multiply(1, y, True)
    lax.fori_loop(1, RING, lambda i, c: (multiply(1, step(y, i), False), c)[1], 0)
    for kind in range(2):
        for head in range(4):
            cols = pl.ds(head * HEAD_WIDTH, HEAD_WIDTH)
            dest = pl.ds((kind * 4 + head) * HEAD_WIDTH, HEAD_WIDTH)
            turned = turn(acc[2 + kind, :, cols], query_gain) * QSCALE ** (-0.5)
            q_ref[:, dest] = turned.astype(BF16)
    for copy in sent:
        copy.wait_send()


def project(tok, gain, wcat, query_gain, key_gain, cosine, sine):
    width, rows = tok.shape
    depth, cols = wcat.shape[1:]
    dma = pltpu.SemaphoreType.DMA
    vmem = pl.BlockSpec(memory_space=pltpu.VMEM)
    return pl.pallas_call(
        project_kernel,
        out_shape=(
            jax.ShapeDtypeStruct((rows, 2 * cols), BF16),
            jax.ShapeDtypeStruct((rows, cols), BF16),
            jax.ShapeDtypeStruct((rows, cols), BF16),
        ),
        in_specs=[vmem, vmem, pl.BlockSpec(memory_space=pl.ANY), vmem, vmem, vmem, vmem],
        out_specs=(vmem, vmem, vmem),
        scratch_shapes=[
            pltpu.VMEM((4, RING, RING, depth, cols), BF16),
            pltpu.VMEM((RING, rows, width), BF16),
            pltpu.VMEM((4, rows, cols), F32),
            pltpu.VMEM((RING, 1, rows), F32),
            dma((2, 8)), dma((2, 8)), dma((2, 4)), dma((2, 4)), dma((2,)),
            dma((3,)), dma((3,)), dma((4,)), dma((4,)),
        ],
        compiler_params=pltpu.CompilerParams(
            collective_id=0, has_side_effects=True, vmem_limit_bytes=58 * 2**20
        ),
        cost_estimate=pl.CostEstimate(
            flops=2 * rows * RING * width * 4 * cols, bytes_accessed=10**8, transcendentals=0
        ),
    )(tok, gain, wcat, query_gain, key_gain, cosine, sine)


def attend_kernel(
    q_ref, k_ref, v_ref, wo_ref,
    out_ref,
    wbuf, kbuf, vbuf, relay, heads, sbuf, rhalf, rfull,
    wsend, wrecv, sib_send, sib_recv, loc, hsend, hrecv, rsend, rrecv,
):
    x, y, z, r = place()
    rows = q_ref.shape[0]
    count = RING * RING
    seq = z * RING + x
    one = 1 - r
    c1 = x * one + z * r
    c2 = z * one + x * r

    def along1(by):
        return device(step(x, by * one), y, step(z, by * r), r)

    def along2(by):
        return device(step(x, by * r), y, step(z, by * one), r)

    def along_y(by):
        return device(x, step(y, by), z, r)

    def at_seq(s):
        return {"seq": s, "hid": y, "rep": r}

    def around(s):
        return lax.rem(s + count, count)

    sibling = device(x, y, z, 1 - r)
    after = at_seq(around(seq + 1))
    before = at_seq(around(seq - 1))
    via = device(step(x, -1), y, z, r)
    via_from = device(step(x, 1), y, z, r)
    onward = at_seq(around(z * RING + step(x, 1) + 2))
    origin = around(seq - 2)
    onward_from = device(step(lax.rem(origin, RING), -1), y, lax.div(origin, RING), r)
    greet([along1(1), along1(-1), along2(1), along2(-1), along_y(1), along_y(-1),
           sibling, after, before, via, via_from, onward, onward_from])

    sent = []

    def go(*args):
        copy = send(*args)
        sent.append(copy)
        return copy

    def slot(i):
        return pl.ds(i * rows, rows)

    h0 = go(k_ref, kbuf.at[slot(1)], hsend.at[0], hrecv.at[0], after)
    h1 = go(v_ref, vbuf.at[slot(1)], hsend.at[1], hrecv.at[1], after)
    h2 = go(v_ref, relay, hsend.at[2], hrecv.at[2], via)

    own = pltpu.make_async_copy(wo_ref.at[r], wbuf.at[r, c2, c1], loc)
    own.start()
    a = [go(wo_ref.at[r], wbuf.at[r, c2, c1], wsend.at[i], wrecv.at[i], along1(by))
         for i, by in enumerate((1, -1))]
    kbuf[slot(2)] = k_ref[...]
    vbuf[slot(2)] = v_ref[...]
    half = wbuf.shape[4] // 2
    b = []
    for i, by in enumerate((1, -1)):
        a[i].wait_recv()
        ref = wbuf.at[r, c2, step(c1, -by), :, pl.ds(i * half, half)]
        b.append(go(ref, ref, wsend.at[2 + i], wrecv.at[2 + i], along1(by)))
    own.wait()
    for copy in b:
        copy.wait_recv()

    def to_sibling(i, row):
        ref = wbuf.at[r, row]
        return go(ref, ref, sib_send.at[i], sib_recv.at[i], sibling)

    ref = wbuf.at[r, c2]
    d = [go(ref, ref, wsend.at[4 + i], wrecv.at[4 + i], along2(by))
         for i, by in enumerate((1, -1))]
    sib = [to_sibling(0, c2)]
    h0.wait_recv()
    h3 = go(kbuf.at[slot(1)], kbuf.at[slot(0)], hsend.at[3], hrecv.at[3], after)
    h2.wait_recv()
    h4 = go(relay, vbuf.at[slot(0)], hsend.at[4], hrecv.at[4], onward)
    e = []
    for i, by in enumerate((1, -1)):
        d[i].wait_recv()
        ref = wbuf.at[r, step(c2, -by), pl.ds(2 * i, 2)]
        e.append(go(ref, ref, wsend.at[6 + i], wrecv.at[6 + i], along2(by)))
    for i, by in enumerate((1, -1)):
        sib.append(to_sibling(1 + i, step(c2, -by)))
    for copy in e:
        copy.wait_recv()
    sib.append(to_sibling(3, step(c2, 2)))

    for copy in (h1, h3, h4):
        copy.wait_recv()
    span = WINDOW + QB
    ri = lax.broadcasted_iota(jnp.int32, (QB, QB), 0)
    ci = lax.broadcasted_iota(jnp.int32, (QB, QB), 1)
    recent = jnp.concatenate([ci <= ri] * 2, axis=0)
    oldest = jnp.concatenate([ci > ri] * 2, axis=0)
    lane = lax.broadcasted_iota(jnp.int32, (1, span), 1)

    def attend(it, carry):
        g = lax.rem(it, RING)
        i = lax.div(it, RING)
        at = pl.multiple_of(i * QB, QB)
        cols = pl.ds(pl.multiple_of(g * HEAD_WIDTH, HEAD_WIDTH), HEAD_WIDTH)
        pair = [pl.ds(pl.multiple_of((2 * g + j) * HEAD_WIDTH, HEAD_WIDTH), HEAD_WIDTH)
                for j in range(2)]
        q = jnp.concatenate([q_ref[pl.ds(at, QB), c] for c in pair], axis=0)
        k = kbuf[pl.ds(at, span), cols]
        v = vbuf[pl.ds(at, span), cols]
        s = lax.dot_general(q, k, (((1,), (1,)), ((), ())), preferred_element_type=F32)
        present = lane + at >= DEPTH * rows - seq * rows
        s = jnp.concatenate([
            jnp.where(oldest, s[:, :QB], -jnp.inf), s[:, QB:WINDOW],
            jnp.where(recent, s[:, WINDOW:], -jnp.inf)], axis=1)
        s = jnp.where(present, s, -jnp.inf)
        p = jnp.exp(s - jnp.max(s, axis=1, keepdims=True))
        p = (p * (1.0 / jnp.sum(p, axis=1, keepdims=True))).astype(BF16)
        o = jnp.dot(p, v, preferred_element_type=F32).astype(BF16)
        for j in range(2):
            heads[pl.ds(at, QB), pair[j]] = o[j * QB:(j + 1) * QB]
        return carry

    lax.fori_loop(0, RING * (rows // QB), attend, 0)
    for copy in sib:
        copy.wait_recv()

    depth = wbuf.shape[3]
    wide = wbuf.shape[4]

    def terms(i, t):
        def one_piece(j, carry):
            part = lax.dot_general(wbuf[0, t, j], heads[:, :wide], (((1,), (1,)), ((), ())),
                                   preferred_element_type=F32)
            part += lax.dot_general(wbuf[1, j, t], heads[:, wide:], (((1,), (1,)), ((), ())),
                                    preferred_element_type=F32)
            sbuf[i, pl.ds(pl.multiple_of(j * depth, 16), depth), :] = part.astype(BF16)
            return carry

        lax.fori_loop(0, RING, one_piece, 0)

    mid = RING * depth // 2
    low, high = pl.ds(0, mid), pl.ds(mid, mid)
    terms(0, step(y, 2))
    f0 = go(sbuf.at[0, low], rhalf.at[0], rsend.at[0], rrecv.at[0], along_y(1))
    f1 = go(sbuf.at[0, high], rhalf.at[1], rsend.at[1], rrecv.at[1], along_y(-1))
    terms(1, step(y, 1))
    g0 = go(sbuf.at[1, high], rfull.at[0, high], rsend.at[2], rrecv.at[2], along_y(1))
    terms(2, step(y, -1))
    g1 = go(sbuf.at[2, low], rfull.at[1, low], rsend.at[3], rrecv.at[3], along_y(-1))
    terms(3, y)
    f0.wait_recv()
    sbuf[1, low, :] = (sbuf[1, low, :].astype(F32) + rhalf[0].astype(F32)).astype(BF16)
    g2 = go(sbuf.at[1, low], rfull.at[0, low], rsend.at[4], rrecv.at[4], along_y(1))
    f1.wait_recv()
    sbuf[2, high, :] = (sbuf[2, high, :].astype(F32) + rhalf[1].astype(F32)).astype(BF16)
    g3 = go(sbuf.at[2, high], rfull.at[1, high], rsend.at[5], rrecv.at[5], along_y(-1))
    for copy in (g0, g1, g2, g3):
        copy.wait_recv()
    out_ref[...] = (sbuf[3].astype(F32) + rfull[0].astype(F32) + rfull[1].astype(F32)).astype(BF16)
    for copy in sent:
        copy.wait_send()


def attend(qh, kh, vh, wo):
    rows = qh.shape[0]
    _, depth, cols = wo.shape
    dma = pltpu.SemaphoreType.DMA
    vmem = pl.BlockSpec(memory_space=pltpu.VMEM)
    return pl.pallas_call(
        attend_kernel,
        out_shape=jax.ShapeDtypeStruct((RING * depth, rows), BF16),
        in_specs=[vmem, vmem, vmem, pl.BlockSpec(memory_space=pl.ANY)],
        out_specs=vmem,
        scratch_shapes=[
            pltpu.VMEM((2, RING, RING, depth, cols), BF16),
            pltpu.VMEM((3 * rows, cols), BF16),
            pltpu.VMEM((3 * rows, cols), BF16),
            pltpu.VMEM((rows, cols), BF16),
            pltpu.VMEM((rows, 2 * cols), BF16),
            pltpu.VMEM((4, RING * depth, rows), BF16),
            pltpu.VMEM((2, RING * depth // 2, rows), BF16),
            pltpu.VMEM((2, RING * depth, rows), BF16),
            dma((8,)), dma((8,)), dma((4,)), dma((4,)), dma,
            dma((5,)), dma((5,)), dma((6,)), dma((6,)),
        ],
        compiler_params=pltpu.CompilerParams(
            collective_id=1, has_side_effects=True, vmem_limit_bytes=58 * 2**20
        ),
    )(qh, kh, vh, wo)


def shards(tokens, norm_gain, w_query, w_key, w_value, query_gain, key_gain, w_out):
    rows, width = tokens.shape
    hid = lax.axis_index("hid")
    gain = lax.dynamic_slice_in_dim(norm_gain, hid * width, width).reshape(width, 1)
    cols = w_key.shape[1]
    wcat = jnp.stack([w_key, w_value, w_query[:, :cols], w_query[:, cols:]])
    base = lax.axis_index("seq") * rows
    qpos = base + jnp.arange(rows, dtype=jnp.int32)
    half = HEAD_WIDTH // 2
    freq = 10000.0 ** (-(jnp.arange(half, dtype=F32) * 2.0) / HEAD_WIDTH)
    angle = qpos.astype(F32)[:, None] * freq[None, :]
    cosine, sine = jnp.cos(angle), jnp.sin(angle)
    qh, kh, value_head = project(
        tokens.T, gain, wcat,
        query_gain.reshape(1, -1), key_gain.reshape(1, -1),
        jnp.concatenate([cosine, cosine], axis=1), jnp.concatenate([-sine, sine], axis=1),
    )
    wo = w_out.T
    wo = jnp.stack([wo[:, :cols], wo[:, cols:]])
    return attend(qh, kh, value_head, wo).T


def solution(mesh):
    return jax.shard_map(
        shards,
        mesh=mesh,
        in_specs=(
            P(("rep", "seq"), "hid"),
            P(),
            P("seq", "hid"),
            P("seq", "hid"),
            P("seq", "hid"),
            P(),
            P(),
            P("hid", "seq"),
        ),
        out_specs=P(("rep", "seq"), "hid"),
        check_vma=False,
    )
```

```python
import functools

import jax
import jax.numpy as jnp
from jax import lax
from jax.experimental import pallas as pl
from jax.experimental.pallas import tpu as pltpu
from jax.sharding import PartitionSpec as P

HEAD_WIDTH = 128
WINDOW = 1024
QSCALE = 168
DEPTH = 2
RING = 4
QB = 128
VMEM_BYTES = 60 * 2**20
MESH = pl.DeviceIdType.MESH
BF16 = jnp.bfloat16
F32 = jnp.float32


def place():
    seq = lax.axis_index("seq")
    return lax.rem(seq, RING), lax.axis_index("hid"), lax.div(seq, RING), lax.axis_index("rep")


def device(x, y, z, r):
    return {"seq": z * RING + x, "hid": y, "rep": r}


def step(a, by):
    return lax.rem(a + by + RING, RING)


def send(src, dst, send_sem, recv_sem, dev):
    copy = pltpu.make_async_remote_copy(
        src_ref=src,
        dst_ref=dst,
        send_sem=send_sem,
        recv_sem=recv_sem,
        device_id=dev,
        device_id_type=MESH,
    )
    copy.start()
    return copy


def greet(devs):
    barrier = pltpu.get_barrier_semaphore()
    for dev in devs:
        pl.semaphore_signal(barrier, inc=1, device_id=dev, device_id_type=MESH)
    pl.semaphore_wait(barrier, len(devs))


class Gather:
    def __init__(self, go, src, buf, c1, c2, along1, along2, sibling, sems):
        self.go, self.src, self.buf, self.c1, self.c2 = go, src, buf, c1, c2
        self.along = (along1, along2)
        self.other = sibling
        self.send, self.recv, self.ssend, self.srecv, self.loc = sems
        self.sib = []

    def piece(self, c2, c1):
        return self.buf.at[c2 * RING + c1]

    def copy(self, src, dst, i, stage, by):
        return self.go(src, dst, self.send.at[i], self.recv.at[i], self.along[stage](by))

    def to_sibling(self, ref):
        if self.other is None:
            return
        i = len(self.sib)
        self.sib.append(self.go(ref, ref, self.ssend.at[i], self.srecv.at[i], self.other))

    def start(self):
        own = self.piece(self.c2, self.c1)
        self.own = pltpu.make_async_copy(self.src, own, self.loc)
        self.own.start()
        self.a = [self.copy(self.src, own, i, 0, by) for i, by in enumerate((1, -1))]

    def pass_first(self):
        half = self.buf.shape[2] // 2
        self.b = []
        for i, by in enumerate((1, -1)):
            self.a[i].wait_recv()
            ref = self.piece(self.c2, step(self.c1, -by)).at[:, pl.ds(i * half, half)]
            self.b.append(self.copy(ref, ref, 2 + i, 0, by))

    def part(self, row, i):
        return self.buf.at[pl.ds(row * RING + 2 * i, 2)]

    def rows(self):
        self.own.wait()
        for copy in self.b:
            copy.wait_recv()
        self.early, self.late = [], []
        for group, flip in ((self.early, 0), (self.late, 1)):
            for i, by in enumerate((1, -1)):
                ref = self.part(self.c2, i ^ flip)
                group.append(self.copy(ref, ref, 4 + 2 * flip + i, 1, by))
        self.to_sibling(self.buf.at[pl.ds(self.c2 * RING, RING)])

    def pass_rows(self):
        self.f = []
        for i, by in enumerate((1, -1)):
            self.early[i].wait_recv()
            ref = self.part(step(self.c2, -by), i)
            self.f.append(self.copy(ref, ref, 8 + i, 1, by))
            self.to_sibling(ref)

    def rest(self):
        for i, by in enumerate((1, -1)):
            self.late[i].wait_recv()
            self.to_sibling(self.part(step(self.c2, -by), 1 - i))

    def last(self):
        for i in range(2):
            self.f[i].wait_recv()
            self.to_sibling(self.part(step(self.c2, 2), i))

    def done(self):
        for copy in self.sib:
            copy.wait_recv()


def block_kernel(
    tok_ref, gain_ref, wcat_ref, wo_ref, qg_ref, kg_ref, cos_ref, sin_ref,
    out_ref,
    wbuf, wobuf, xbuf, acc, sums, kvbuf, relay, heads, others, sbuf, rhalf, rfull,
    wsend, wrecv, sib_send, sib_recv, loc, tok_sem,
    ssend, srecv, xsend, xrecv, xssend, xsrecv, hsend, hrecv, osend, orecv, rsend, rrecv,
):
    x, y, z, r = place()
    width, rows = tok_ref.shape
    count = RING * RING
    seq = z * RING + x
    one = 1 - r

    def along1(by):
        return device(step(x, by * one), y, step(z, by * r), r)

    def along2(by):
        return device(step(x, by * r), y, step(z, by * one), r)

    def along_x(by):
        return device(step(x, by), y, z, r)

    def along_y(by):
        return device(x, step(y, by), z, r)

    def along_z(by):
        return device(x, y, step(z, by), r)

    def at_seq(s):
        return {"seq": s, "hid": y, "rep": r}

    def around(s):
        return lax.rem(s + count, count)

    sibling = device(x, y, z, 1 - r)
    after = at_seq(around(seq + 1))
    before = at_seq(around(seq - 1))
    onward = at_seq(around(z * RING + step(x, 1) + 2))
    origin = around(seq - 2)
    onward_from = device(step(lax.rem(origin, RING), -1), y, lax.div(origin, RING), r)
    greet([along_x(1), along_x(-1), along_z(1), along_z(-1),
           along_y(1), along_y(-1), along_y(2),
           sibling, after, before, onward, onward_from])

    sent = []

    def go(*args):
        copy = send(*args)
        sent.append(copy)
        return copy

    def sems(ph):
        return wsend.at[ph], wrecv.at[ph], sib_send, sib_recv, loc.at[ph]

    c1, c2 = x * one + z * r, z * one + x * r
    kv, qq = (Gather(go, wcat_ref.at[ph], wbuf.at[ph], c1, c2, along1, along2, None, sems(ph))
              for ph in range(2))
    oo = Gather(go, wo_ref, wobuf.at[r], c1, c2, along1, along2, sibling, sems(2))

    tok = sbuf.at[0]
    fetch = pltpu.make_async_copy(tok_ref, tok, tok_sem)
    fetch.start()
    kv.start()
    fetch.wait()

    raw = tok[...].astype(F32)
    sums[y] = jnp.sum(raw * raw, axis=0, keepdims=True)
    told = [go(sums.at[y], sums.at[y], ssend.at[i], srecv.at[i], along_y(by))
            for i, by in enumerate((1, 2, 3))]
    kv.pass_first()
    qq.start()
    for copy in told:
        copy.wait_recv()
    total = sums[0] + sums[1] + sums[2] + sums[3]
    scale = lax.rsqrt(total * (1.0 / (RING * width)) + 1e-06)

    def norm_chunk(at, size):
        part = tok[pl.ds(at, size), :].astype(F32)
        part = part * scale * gain_ref[pl.ds(at, size), :]
        xbuf[r, y, :, pl.ds(at, size)] = part.T.astype(BF16)

    lanes = 128

    def norm_step(i, carry):
        norm_chunk(pl.multiple_of(i * lanes, lanes), lanes)
        return carry

    lax.fori_loop(0, width // lanes, norm_step, 0)
    if width % lanes:
        norm_chunk(width // lanes * lanes, width % lanes)

    def x_part(block, i):
        return xbuf.at[r, block, pl.ds(i * (rows // 2), rows // 2)]

    x_sib = []

    def x_over(ref):
        i = len(x_sib)
        x_sib.append(go(ref, ref, xssend.at[i], xsrecv.at[i], sibling))

    x_early, x_late = [], []
    for group, flip in ((x_early, 0), (x_late, 1)):
        for i, by in enumerate((1, -1)):
            ref = x_part(y, i ^ flip)
            group.append(go(ref, ref, xsend.at[2 * flip + i], xrecv.at[2 * flip + i], along_y(by)))

    x_over(xbuf.at[r, y])
    kv.rows()
    qq.pass_first()
    oo.start()
    qq.rows()
    oo.pass_first()
    kv.pass_rows()
    x_last = []
    for i, by in enumerate((1, -1)):
        x_early[i].wait_recv()
        ref = x_part(step(y, -by), i)
        x_last.append(go(ref, ref, xsend.at[4 + i], xrecv.at[4 + i], along_y(by)))
        x_over(ref)
    kv.rest()
    qq.pass_rows()
    kv.last()

    def slots(kind, t, j):
        low = 1 - kind
        return t * (RING * low + kind) + j * (low + RING * kind)

    def multiply(ph, h, first):
        right = jnp.concatenate([wbuf[ph, slots(r, h, j)] for j in range(RING)], axis=0)
        for side in range(2):
            part = jnp.dot(xbuf[side, h], right, preferred_element_type=F32)
            if first:
                acc[side] = part
            else:
                acc[side] += part

    x_sib[0].wait_recv()
    multiply(0, y, True)
    for i, by in enumerate((1, -1)):
        x_late[i].wait_recv()
        x_over(x_part(step(y, -by), 1 - i))
    qq.rest()
    for copy in x_sib[1:]:
        copy.wait_recv()
    lax.fori_loop(0, 2, lambda i, c: (multiply(0, step(y, 1 + 2 * i), False), c)[1], 0)
    for i in range(2):
        x_last[i].wait_recv()
        x_over(x_part(step(y, 2), i))
    for copy in x_sib[5:]:
        copy.wait_recv()
    multiply(0, step(y, 2), False)

    cosine, sine = cos_ref[...], sin_ref[...]

    def turn(u, gain):
        u = u * lax.rsqrt(jnp.mean(u * u, axis=-1, keepdims=True) + 1e-06) * gain
        return u * cosine + pltpu.roll(u, HEAD_WIDTH // 2, 1) * sine

    def slot(i):
        return pl.ds(i * rows, rows)

    key_gain, query_gain = kg_ref[...], qg_ref[...]
    pair_width = 2 * HEAD_WIDTH

    def keys_values(side, carry):
        for head in range(2):
            cols = pl.ds(head * HEAD_WIDTH, HEAD_WIDTH)
            kvbuf[side, slot(2), cols] = turn(acc[side, :, cols], key_gain).astype(BF16)
        cols = pl.ds(pair_width, pair_width)
        kvbuf[side, slot(2), cols] = acc[side, :, cols].astype(BF16)
        return carry

    lax.fori_loop(0, 2, keys_values, 0)
    h0 = go(kvbuf.at[0, slot(2)], kvbuf.at[0, slot(1)], hsend.at[0], hrecv.at[0], after)
    h2 = go(kvbuf.at[1, slot(2)], relay, hsend.at[2], hrecv.at[2], along_x(-1))
    h1 = go(kvbuf.at[1, slot(2)], kvbuf.at[1, slot(1)], hsend.at[1], hrecv.at[1], after)

    oo.rows()
    qq.last()
    multiply(1, y, True)
    lax.fori_loop(1, RING, lambda i, c: (multiply(1, step(y, i), False), c)[1], 0)

    def queries(side, carry):
        for head in range(4):
            cols = pl.ds(head * HEAD_WIDTH, HEAD_WIDTH)
            turned = turn(acc[side, :, cols], query_gain) * QSCALE ** (-0.5)
            heads[side, :, cols] = turned.astype(BF16)
        return carry

    lax.fori_loop(0, 2, queries, 0)
    h0.wait_recv()
    h3 = go(kvbuf.at[0, slot(1)], kvbuf.at[0, slot(0)], hsend.at[3], hrecv.at[3], after)
    h2.wait_recv()
    h4 = go(relay, kvbuf.at[1, slot(0)], hsend.at[4], hrecv.at[4], onward)
    oo.pass_rows()
    oo.rest()
    for copy in (h1, h3, h4):
        copy.wait_recv()

    span = WINDOW + QB
    ri = lax.broadcasted_iota(jnp.int32, (QB, QB), 0)
    ci = lax.broadcasted_iota(jnp.int32, (QB, QB), 1)
    recent = jnp.concatenate([ci <= ri] * 2, axis=0)
    oldest = jnp.concatenate([ci > ri] * 2, axis=0)
    lane = lax.broadcasted_iota(jnp.int32, (1, span), 1)

    def attend(side, it):
        g = lax.rem(it, 2)
        i = lax.div(it, 2)
        at = pl.multiple_of(i * QB, QB)
        k_cols = pl.ds(pl.multiple_of(g * HEAD_WIDTH, HEAD_WIDTH), HEAD_WIDTH)
        v_cols = pl.ds(pl.multiple_of((2 + g) * HEAD_WIDTH, HEAD_WIDTH), HEAD_WIDTH)
        pair = [pl.ds(pl.multiple_of((2 * g + j) * HEAD_WIDTH, HEAD_WIDTH), HEAD_WIDTH)
                for j in range(2)]
        q = jnp.concatenate([heads[side, pl.ds(at, QB), c] for c in pair], axis=0)
        k = kvbuf[side, pl.ds(at, span), k_cols]
        v = kvbuf[side, pl.ds(at, span), v_cols]
        s = lax.dot_general(q, k, (((1,), (1,)), ((), ())), preferred_element_type=F32)
        present = lane + at >= DEPTH * rows - seq * rows
        s = jnp.concatenate([
            jnp.where(oldest, s[:, :QB], -jnp.inf), s[:, QB:WINDOW],
            jnp.where(recent, s[:, WINDOW:], -jnp.inf)], axis=1)
        s = jnp.where(present, s, -jnp.inf)
        p = jnp.exp(s - jnp.max(s, axis=1, keepdims=True))
        p = (p * (1.0 / jnp.sum(p, axis=1, keepdims=True))).astype(BF16)
        o = jnp.dot(p, v, preferred_element_type=F32).astype(BF16)
        for j in range(2):
            heads[side, pl.ds(at, QB), pair[j]] = o[j * QB:(j + 1) * QB]

    def attend_all(side):
        lax.fori_loop(0, 2 * (rows // QB), lambda it, c: (attend(side, it), c)[1], 0)

    attend_all(1 - r)
    swap = go(heads.at[1 - r], others, osend, orecv, sibling)
    attend_all(r)
    oo.last()
    swap.wait_recv()
    oo.done()

    depth = wobuf.shape[2]

    def terms(dest, t):
        def one_piece(j, carry):
            part = lax.dot_general(wobuf[r, slots(r, t, j)], heads[r], (((1,), (1,)), ((), ())),
                                   preferred_element_type=F32)
            part += lax.dot_general(wobuf[1 - r, slots(1 - r, t, j)], others[...],
                                    (((1,), (1,)), ((), ())), preferred_element_type=F32)
            dest[pl.ds(pl.multiple_of(j * depth, 16), depth), :] = part.astype(BF16)
            return carry

        lax.fori_loop(0, RING, one_piece, 0)

    mid = RING * depth // 2
    low, high = pl.ds(0, mid), pl.ds(mid, mid)
    terms(sbuf.at[0], step(y, 2))
    f0 = go(sbuf.at[0, low], rhalf.at[0], rsend.at[0], rrecv.at[0], along_y(1))
    f1 = go(sbuf.at[0, high], rhalf.at[1], rsend.at[1], rrecv.at[1], along_y(-1))
    terms(sbuf.at[1], step(y, 1))
    g0 = go(sbuf.at[1, high], rfull.at[0, high], rsend.at[2], rrecv.at[2], along_y(1))
    terms(sbuf.at[2], step(y, -1))
    g1 = go(sbuf.at[2, low], rfull.at[1, low], rsend.at[3], rrecv.at[3], along_y(-1))
    terms(out_ref, y)
    f0.wait_recv()
    sbuf[1, low, :] = (sbuf[1, low, :].astype(F32) + rhalf[0].astype(F32)).astype(BF16)
    g2 = go(sbuf.at[1, low], rfull.at[0, low], rsend.at[4], rrecv.at[4], along_y(1))
    f1.wait_recv()
    sbuf[2, high, :] = (sbuf[2, high, :].astype(F32) + rhalf[1].astype(F32)).astype(BF16)
    g3 = go(sbuf.at[2, high], rfull.at[1, high], rsend.at[5], rrecv.at[5], along_y(-1))
    for copy in (g0, g1, g2, g3):
        copy.wait_recv()
    out_ref[...] = (out_ref[...].astype(F32) + rfull[0].astype(F32) + rfull[1].astype(F32)).astype(BF16)
    for copy in sent:
        copy.wait_send()


def block(tok, gain, wcat, wo, query_gain, key_gain, cosine, sine):
    width, rows = tok.shape
    _, depth, cols = wcat.shape
    dma = pltpu.SemaphoreType.DMA
    vmem = pl.BlockSpec(memory_space=pltpu.VMEM)
    hbm = pl.BlockSpec(memory_space=pl.ANY)
    return pl.pallas_call(
        block_kernel,
        out_shape=jax.ShapeDtypeStruct((width, rows), BF16),
        in_specs=[hbm, vmem, hbm, hbm, vmem, vmem, vmem, vmem],
        out_specs=vmem,
        scratch_shapes=[
            pltpu.VMEM((2, RING * RING, depth, cols), BF16),
            pltpu.VMEM((2, RING * RING, depth, cols), BF16),
            pltpu.VMEM((2, RING, rows, width), BF16),
            pltpu.VMEM((2, rows, cols), F32),
            pltpu.VMEM((RING, 1, rows), F32),
            pltpu.VMEM((2, 3 * rows, cols), BF16),
            pltpu.VMEM((rows, cols), BF16),
            pltpu.VMEM((2, rows, cols), BF16),
            pltpu.VMEM((rows, cols), BF16),
            pltpu.VMEM((3, width, rows), BF16),
            pltpu.VMEM((2, width // 2, rows), BF16),
            pltpu.VMEM((2, width, rows), BF16),
            dma((3, 10)), dma((3, 10)), dma((7,)), dma((7,)), dma((3,)), dma,
            dma((3,)), dma((3,)), dma((6,)), dma((6,)), dma((7,)), dma((7,)),
            dma((5,)), dma((5,)), dma, dma, dma((6,)), dma((6,)),
        ],
        compiler_params=pltpu.CompilerParams(
            collective_id=0, has_side_effects=True, vmem_limit_bytes=VMEM_BYTES
        ),
    )(tok, gain, wcat, wo, query_gain, key_gain, cosine, sine)


def shards(tokens, norm_gain, w_query, w_key, w_value, query_gain, key_gain, w_out):
    rows, width = tokens.shape
    hid = lax.axis_index("hid")
    gain = lax.dynamic_slice_in_dim(norm_gain, hid * width, width).reshape(width, 1)
    core = lax.axis_index("rep")

    def of_core(a, axis):
        half = a.shape[axis] // 2
        return lax.dynamic_slice_in_dim(a, core * half, half, axis)

    wcat = jnp.stack([
        jnp.concatenate([of_core(w_key, 1), of_core(w_value, 1)], axis=1), of_core(w_query, 1)
    ])
    wo = of_core(w_out, 0).T
    base = lax.axis_index("seq") * rows
    qpos = base + jnp.arange(rows, dtype=jnp.int32)
    half = HEAD_WIDTH // 2
    freq = 10000.0 ** (-(jnp.arange(half, dtype=F32) * 2.0) / HEAD_WIDTH)
    angle = qpos.astype(F32)[:, None] * freq[None, :]
    cosine, sine = jnp.cos(angle), jnp.sin(angle)
    return block(
        tokens.T, gain, wcat, wo,
        query_gain.reshape(1, -1), key_gain.reshape(1, -1),
        jnp.concatenate([cosine, cosine], axis=1), jnp.concatenate([-sine, sine], axis=1),
    ).T


def solution(mesh):
    return jax.shard_map(
        shards,
        mesh=mesh,
        in_specs=(
            P(("rep", "seq"), "hid"),
            P(),
            P("seq", "hid"),
            P("seq", "hid"),
            P("seq", "hid"),
            P(),
            P(),
            P("hid", "seq"),
        ),
        out_specs=P(("rep", "seq"), "hid"),
        check_vma=False,
    )
```

```python
import functools

import jax
import jax.numpy as jnp
from jax import lax
from jax.experimental import pallas as pl
from jax.experimental.pallas import tpu as pltpu
from jax.sharding import PartitionSpec as P

HEAD_WIDTH = 128
WINDOW = 1024
QSCALE = 168
DEPTH = 2
RING = 4
QB = 128
VMEM_BYTES = 60 * 2**20
MESH = pl.DeviceIdType.MESH
BF16 = jnp.bfloat16
F32 = jnp.float32


def place():
    seq = lax.axis_index("seq")
    return lax.rem(seq, RING), lax.axis_index("hid"), lax.div(seq, RING), lax.axis_index("rep")


def device(x, y, z, r):
    return {"seq": z * RING + x, "hid": y, "rep": r}


def step(a, by):
    return lax.rem(a + by + RING, RING)


def send(src, dst, send_sem, recv_sem, dev):
    copy = pltpu.make_async_remote_copy(
        src_ref=src,
        dst_ref=dst,
        send_sem=send_sem,
        recv_sem=recv_sem,
        device_id=dev,
        device_id_type=MESH,
    )
    copy.start()
    return copy


def greet(devs):
    barrier = pltpu.get_barrier_semaphore()
    for dev in devs:
        pl.semaphore_signal(barrier, inc=1, device_id=dev, device_id_type=MESH)
    pl.semaphore_wait(barrier, len(devs))


class Gather:
    def __init__(self, go, src, buf, c1, c2, along1, along2, sibling, sems):
        self.go, self.src, self.buf, self.c1, self.c2 = go, src, buf, c1, c2
        self.along = (along1, along2)
        self.other = sibling
        self.send, self.recv, self.ssend, self.srecv, self.loc = sems
        self.sib = []

    def piece(self, c2, c1):
        return self.buf.at[c2 * RING + c1]

    def copy(self, src, dst, i, stage, by):
        return self.go(src, dst, self.send.at[i], self.recv.at[i], self.along[stage](by))

    def to_sibling(self, ref):
        if self.other is None:
            return
        i = len(self.sib)
        self.sib.append(self.go(ref, ref, self.ssend.at[i], self.srecv.at[i], self.other))

    def start(self):
        own = self.piece(self.c2, self.c1)
        self.own = pltpu.make_async_copy(self.src, own, self.loc)
        self.own.start()
        self.a = [self.copy(self.src, own, i, 0, by) for i, by in enumerate((1, -1))]

    def pass_first(self):
        half = self.buf.shape[2] // 2
        self.b = []
        for i, by in enumerate((1, -1)):
            self.a[i].wait_recv()
            ref = self.piece(self.c2, step(self.c1, -by)).at[:, pl.ds(i * half, half)]
            self.b.append(self.copy(ref, ref, 2 + i, 0, by))

    def part(self, row, i):
        return self.buf.at[pl.ds(row * RING + 2 * i, 2)]

    def rows(self):
        self.own.wait()
        for copy in self.b:
            copy.wait_recv()
        self.early, self.late = [], []
        for group, flip in ((self.early, 0), (self.late, 1)):
            for i, by in enumerate((1, -1)):
                ref = self.part(self.c2, i ^ flip)
                group.append(self.copy(ref, ref, 4 + 2 * flip + i, 1, by))
        self.to_sibling(self.buf.at[pl.ds(self.c2 * RING, RING)])

    def pass_rows(self):
        self.f = []
        for i, by in enumerate((1, -1)):
            self.early[i].wait_recv()
            ref = self.part(step(self.c2, -by), i)
            self.f.append(self.copy(ref, ref, 8 + i, 1, by))
            self.to_sibling(ref)

    def rest(self):
        for i, by in enumerate((1, -1)):
            self.late[i].wait_recv()
            self.to_sibling(self.part(step(self.c2, -by), 1 - i))

    def last(self):
        for i in range(2):
            self.f[i].wait_recv()
            self.to_sibling(self.part(step(self.c2, 2), i))

    def done(self):
        for copy in self.sib:
            copy.wait_recv()


def block_kernel(
    tok_ref, gain_ref, wcat_ref, wo_ref, qg_ref, kg_ref, cos_ref, sin_ref,
    out_ref,
    tokbuf, wbuf, wo_a, wo_b, xbuf, acc, sums, kvbuf, relay, heads, others, sbuf, rhalf, rfull,
    wsend, wrecv, sib_send, sib_recv, loc, tok_sem,
    ssend, srecv, xsend, xrecv, xssend, xsrecv, hsend, hrecv, osend, orecv, rsend, rrecv,
):
    x, y, z, r = place()
    width, rows = tok_ref.shape
    count = RING * RING
    seq = z * RING + x
    one = 1 - r

    def along1(by):
        return device(step(x, by * one), y, step(z, by * r), r)

    def along2(by):
        return device(step(x, by * r), y, step(z, by * one), r)

    def along_x(by):
        return device(step(x, by), y, z, r)

    def along_y(by):
        return device(x, step(y, by), z, r)

    def along_z(by):
        return device(x, y, step(z, by), r)

    def at_seq(s):
        return {"seq": s, "hid": y, "rep": r}

    def around(s):
        return lax.rem(s + count, count)

    sibling = device(x, y, z, 1 - r)
    after = at_seq(around(seq + 1))
    before = at_seq(around(seq - 1))
    via = device(step(x, -1), y, step(z, lax.div(x + 2, RING)), r)
    back = step(x, 1)
    via_from = device(back, y, step(z, -lax.div(back + 2, RING)), r)
    greet([along_x(1), along_x(-1), along_z(1), along_z(-1),
           along_y(1), along_y(-1), along_y(2),
           sibling, after, before, via, via_from])

    sent = []

    def go(*args):
        copy = send(*args)
        sent.append(copy)
        return copy

    def sems(ph):
        side = max(ph - 2, 0)
        return wsend.at[ph], wrecv.at[ph], sib_send.at[side], sib_recv.at[side], loc.at[ph]

    c1, c2 = x * one + z * r, z * one + x * r
    kv, qq = (Gather(go, wcat_ref.at[ph], wbuf.at[ph], c1, c2, along1, along2, None, sems(ph))
              for ph in range(2))
    outs = []
    for n, buf in enumerate((wo_a, wo_b)):
        at = pl.ds(n * wo_a.shape[2], buf.shape[2])
        outs.append(Gather(go, wo_ref.at[at], buf.at[r], c1, c2, along1, along2, sibling,
                           sems(2 + n)))
    oa, ob = outs

    tok = tokbuf
    fetch = pltpu.make_async_copy(tok_ref, tok, tok_sem)
    fetch.start()
    kv.start()
    fetch.wait()

    raw = tok[...].astype(F32)
    sums[y] = jnp.sum(raw * raw, axis=0, keepdims=True)
    told = [go(sums.at[y], sums.at[y], ssend.at[i], srecv.at[i], along_y(by))
            for i, by in enumerate((1, 2, 3))]
    kv.pass_first()
    qq.start()
    for copy in told:
        copy.wait_recv()
    total = sums[0] + sums[1] + sums[2] + sums[3]
    scale = lax.rsqrt(total * (1.0 / (RING * width)) + 1e-06)

    lanes = 128
    chunk = rows // 2
    part_rows = chunk // 2

    def rows_of(c):
        return pl.ds(c * chunk, chunk)

    def norm(c):
        mine = scale[:, c * chunk:(c + 1) * chunk]

        def norm_at(at, size):
            part = tok[pl.ds(at, size), rows_of(c)].astype(F32)
            part = part * mine * gain_ref[pl.ds(at, size), :]
            xbuf[r, y, rows_of(c), pl.ds(at, size)] = part.T.astype(BF16)

        def norm_step(i, carry):
            norm_at(pl.multiple_of(i * lanes, lanes), lanes)
            return carry

        lax.fori_loop(0, width // lanes, norm_step, 0)
        if width % lanes:
            norm_at(width // lanes * lanes, width % lanes)

    def x_part(block, i):
        return xbuf.at[r, block, pl.ds(i * part_rows, part_rows)]

    x_early, x_late, x_last, x_sib = {}, {}, {}, {0: [], 1: []}

    def x_over(c, ref):
        i = 7 * c + len(x_sib[c])
        x_sib[c].append(go(ref, ref, xssend.at[i], xsrecv.at[i], sibling))

    def x_send(c):
        for flip, group in enumerate((x_early, x_late)):
            group[c] = []
            for i, by in enumerate((1, -1)):
                ref = x_part(y, 2 * c + (i ^ flip))
                at = 6 * c + 2 * flip + i
                group[c].append(go(ref, ref, xsend.at[at], xrecv.at[at], along_y(by)))
        x_over(c, xbuf.at[r, y, rows_of(c)])

    def x_pass(c):
        x_last[c] = []
        for i, by in enumerate((1, -1)):
            x_early[c][i].wait_recv()
            ref = x_part(step(y, -by), 2 * c + i)
            at = 6 * c + 4 + i
            x_last[c].append(go(ref, ref, xsend.at[at], xrecv.at[at], along_y(by)))
            x_over(c, ref)

    def x_rest(c):
        for i, by in enumerate((1, -1)):
            x_late[c][i].wait_recv()
            x_over(c, x_part(step(y, -by), 2 * c + 1 - i))

    def x_end(c):
        for i in range(2):
            x_last[c][i].wait_recv()
            x_over(c, x_part(step(y, 2), 2 * c + i))

    def slots(kind, t, j):
        low = 1 - kind
        return t * (RING * low + kind) + j * (low + RING * kind)

    def multiply(ph, h, at, first):
        right = jnp.concatenate([wbuf[ph, slots(r, h, j)] for j in range(RING)], axis=0)
        for side in range(2):
            part = jnp.dot(xbuf[side, h, at], right, preferred_element_type=F32)
            if first:
                acc[side, at] = part
            else:
                acc[side, at] += part

    def turn(u, gain, at):
        u = u * lax.rsqrt(jnp.mean(u * u, axis=-1, keepdims=True) + 1e-06) * gain
        return u * cos_ref[at] + pltpu.roll(u, HEAD_WIDTH // 2, 1) * sin_ref[at]

    key_gain, query_gain = kg_ref[...], qg_ref[...]
    pair_width = 2 * HEAD_WIDTH

    def block_rows(i, c):
        return pl.ds(i * rows + c * chunk, chunk)

    def keys_values(c):
        at = rows_of(c)

        def of_side(side, carry):
            for head in range(2):
                cols = pl.ds(head * HEAD_WIDTH, HEAD_WIDTH)
                kvbuf[side, block_rows(2, c), cols] = turn(acc[side, at, cols], key_gain, at).astype(BF16)
            cols = pl.ds(pair_width, pair_width)
            kvbuf[side, block_rows(2, c), cols] = acc[side, at, cols].astype(BF16)
            return carry

        lax.fori_loop(0, 2, of_side, 0)

    halo = {}

    def halo_go(c, i, src, dst, dev):
        halo[c, i] = go(src, dst, hsend.at[5 * c + i], hrecv.at[5 * c + i], dev)

    def halo_send(c):
        own0, own1 = (kvbuf.at[side, block_rows(2, c)] for side in range(2))
        halo_go(c, 0, own0, kvbuf.at[0, block_rows(1, c)], after)
        halo_go(c, 2, own1, relay.at[c], via)
        halo_go(c, 1, own1, kvbuf.at[1, block_rows(1, c)], after)

    def halo_pass(c):
        halo[c, 0].wait_recv()
        halo_go(c, 3, kvbuf.at[0, block_rows(1, c)], kvbuf.at[0, block_rows(0, c)], after)
        halo[c, 2].wait_recv()
        halo_go(c, 4, relay.at[c], kvbuf.at[1, block_rows(0, c)], along_x(-1))

    norm(1)
    x_send(1)
    kv.rows()
    qq.pass_first()
    norm(0)
    x_pass(1)
    x_send(0)
    kv.pass_rows()
    qq.rows()
    x_rest(1)
    kv.rest()
    oa.start()
    ob.start()
    x_end(1)
    kv.last()
    oa.pass_first()
    ob.pass_first()
    for copy in x_sib[1]:
        copy.wait_recv()
    multiply(0, y, rows_of(1), True)
    lax.fori_loop(1, RING, lambda i, c: (multiply(0, step(y, i), rows_of(1), False), c)[1], 0)
    keys_values(1)
    halo_send(1)
    x_pass(0)
    qq.pass_rows()
    x_rest(0)
    for copy in x_sib[0]:
        copy.wait_recv()
    multiply(0, y, rows_of(0), True)
    halo_pass(1)
    lax.fori_loop(0, 2, lambda i, c: (multiply(0, step(y, 1 + 2 * i), rows_of(0), False), c)[1], 0)
    x_end(0)
    for copy in x_sib[0][5:]:
        copy.wait_recv()
    multiply(0, step(y, 2), rows_of(0), False)
    keys_values(0)
    halo_send(0)
    qq.rest()
    qq.last()
    whole = pl.ds(0, rows)
    multiply(1, y, whole, True)
    lax.fori_loop(1, RING, lambda i, c: (multiply(1, step(y, i), whole, False), c)[1], 0)

    def queries(side, carry):
        for head in range(4):
            cols = pl.ds(head * HEAD_WIDTH, HEAD_WIDTH)
            turned = turn(acc[side, :, cols], query_gain, whole) * QSCALE ** (-0.5)
            heads[side, :, cols] = turned.astype(BF16)
        return carry

    lax.fori_loop(0, 2, queries, 0)
    halo_pass(0)
    oa.rows()
    for c in (1, 0):
        for i in (1, 3, 4):
            halo[c, i].wait_recv()

    span = WINDOW + QB
    ri = lax.broadcasted_iota(jnp.int32, (QB, QB), 0)
    ci = lax.broadcasted_iota(jnp.int32, (QB, QB), 1)
    recent = jnp.concatenate([ci <= ri] * 2, axis=0)
    oldest = jnp.concatenate([ci > ri] * 2, axis=0)
    lane = lax.broadcasted_iota(jnp.int32, (1, span), 1)

    def attend(side, it):
        g = lax.rem(it, 2)
        i = lax.div(it, 2)
        at = pl.multiple_of(i * QB, QB)
        k_cols = pl.ds(pl.multiple_of(g * HEAD_WIDTH, HEAD_WIDTH), HEAD_WIDTH)
        v_cols = pl.ds(pl.multiple_of((2 + g) * HEAD_WIDTH, HEAD_WIDTH), HEAD_WIDTH)
        pair = [pl.ds(pl.multiple_of((2 * g + j) * HEAD_WIDTH, HEAD_WIDTH), HEAD_WIDTH)
                for j in range(2)]
        q = jnp.concatenate([heads[side, pl.ds(at, QB), c] for c in pair], axis=0)
        k = kvbuf[side, pl.ds(at, span), k_cols]
        v = kvbuf[side, pl.ds(at, span), v_cols]
        s = lax.dot_general(q, k, (((1,), (1,)), ((), ())), preferred_element_type=F32)
        present = lane + at >= DEPTH * rows - seq * rows
        s = jnp.concatenate([
            jnp.where(oldest, s[:, :QB], -jnp.inf), s[:, QB:WINDOW],
            jnp.where(recent, s[:, WINDOW:], -jnp.inf)], axis=1)
        s = jnp.where(present, s, -jnp.inf)
        p = jnp.exp(s - jnp.max(s, axis=1, keepdims=True))
        p = (p * (1.0 / jnp.sum(p, axis=1, keepdims=True))).astype(BF16)
        o = jnp.dot(p, v, preferred_element_type=F32).astype(BF16)
        for j in range(2):
            heads[side, pl.ds(at, QB), pair[j]] = o[j * QB:(j + 1) * QB]

    def attend_all(side):
        lax.fori_loop(0, 2 * (rows // QB), lambda it, c: (attend(side, it), c)[1], 0)

    attend_all(1 - r)
    swap = go(heads.at[1 - r], others, osend, orecv, sibling)
    oa.pass_rows()
    ob.rows()
    attend_all(r)
    oa.rest()
    oa.last()
    swap.wait_recv()

    depth = wo_a.shape[2] + wo_b.shape[2]
    near, far = pl.ds(0, chunk), pl.ds(chunk, chunk)
    flows = {}

    def terms(n, t, dest):
        buf = (wo_a, wo_b)[n]
        start, size = n * wo_a.shape[2], buf.shape[2]

        def one_piece(j, carry):
            part = lax.dot_general(buf[r, slots(r, t, j)], heads[r], (((1,), (1,)), ((), ())),
                                   preferred_element_type=F32)
            part += lax.dot_general(buf[1 - r, slots(1 - r, t, j)], others[...],
                                    (((1,), (1,)), ((), ())), preferred_element_type=F32)
            dest[j, pl.ds(start, size), :] = part.astype(BF16)
            return carry

        lax.fori_loop(0, RING, one_piece, 0)

    def cut(n):
        return pl.ds(n * wo_a.shape[2], (wo_a, wo_b)[n].shape[2])

    def flow(n, i, src, dst, by):
        flows[n, i] = go(src, dst, rsend.at[6 * n + i], rrecv.at[6 * n + i], along_y(by))

    def spread(n):
        at = cut(n)
        terms(n, step(y, 2), sbuf.at[0])
        flow(n, 0, sbuf.at[0, :, at, near], rhalf.at[0, :, at], 1)
        flow(n, 1, sbuf.at[0, :, at, far], rhalf.at[1, :, at], -1)
        terms(n, step(y, 1), sbuf.at[1])
        flow(n, 2, sbuf.at[1, :, at, far], rfull.at[0, :, at, far], 1)
        terms(n, step(y, -1), sbuf.at[2])
        flow(n, 3, sbuf.at[2, :, at, near], rfull.at[1, :, at, near], -1)

    def add(n):
        at = cut(n)
        for i, half, by in ((0, near, 1), (1, far, -1)):
            flows[n, i].wait_recv()
            both = sbuf[1 + i, :, at, half].astype(F32) + rhalf[i, :, at].astype(F32)
            sbuf[1 + i, :, at, half] = both.astype(BF16)
            flow(n, 4 + i, sbuf.at[1 + i, :, at, half], rfull.at[i, :, at, half], by)

    def close(n):
        at = cut(n)
        for i in range(2, 6):
            flows[n, i].wait_recv()
        out_ref[:, at, :] = (out_ref[:, at, :].astype(F32) + rfull[0, :, at, :].astype(F32)
                             + rfull[1, :, at, :].astype(F32)).astype(BF16)

    oa.done()
    spread(0)
    ob.pass_rows()
    terms(0, y, out_ref)
    add(0)
    ob.rest()
    ob.last()
    ob.done()
    spread(1)
    terms(1, y, out_ref)
    add(1)
    close(0)
    close(1)
    for copy in sent:
        copy.wait_send()


def block(tok, gain, wcat, wo, query_gain, key_gain, cosine, sine):
    width, rows = tok.shape
    _, depth, cols = wcat.shape
    first = -(-depth // 32) * 16
    dma = pltpu.SemaphoreType.DMA
    vmem = pl.BlockSpec(memory_space=pltpu.VMEM)
    hbm = pl.BlockSpec(memory_space=pl.ANY)
    return pl.pallas_call(
        block_kernel,
        out_shape=jax.ShapeDtypeStruct((RING, depth, rows), BF16),
        in_specs=[hbm, vmem, hbm, hbm, vmem, vmem, vmem, vmem],
        out_specs=vmem,
        scratch_shapes=[
            pltpu.VMEM((width, rows), BF16),
            pltpu.VMEM((2, RING * RING, depth, cols), BF16),
            pltpu.VMEM((2, RING * RING, first, cols), BF16),
            pltpu.VMEM((2, RING * RING, depth - first, cols), BF16),
            pltpu.VMEM((2, RING, rows, width), BF16),
            pltpu.VMEM((2, rows, cols), F32),
            pltpu.VMEM((RING, 1, rows), F32),
            pltpu.VMEM((2, 3 * rows, cols), BF16),
            pltpu.VMEM((2, rows // 2, cols), BF16),
            pltpu.VMEM((2, rows, cols), BF16),
            pltpu.VMEM((rows, cols), BF16),
            pltpu.VMEM((3, RING, depth, rows), BF16),
            pltpu.VMEM((2, RING, depth, rows // 2), BF16),
            pltpu.VMEM((2, RING, depth, rows), BF16),
            dma((4, 10)), dma((4, 10)), dma((2, 7)), dma((2, 7)), dma((4,)), dma,
            dma((3,)), dma((3,)), dma((12,)), dma((12,)), dma((14,)), dma((14,)),
            dma((10,)), dma((10,)), dma, dma, dma((12,)), dma((12,)),
        ],
        compiler_params=pltpu.CompilerParams(
            collective_id=0, has_side_effects=True, vmem_limit_bytes=VMEM_BYTES
        ),
    )(tok, gain, wcat, wo, query_gain, key_gain, cosine, sine)


def shards(tokens, norm_gain, w_query, w_key, w_value, query_gain, key_gain, w_out):
    rows, width = tokens.shape
    hid = lax.axis_index("hid")
    gain = lax.dynamic_slice_in_dim(norm_gain, hid * width, width).reshape(width, 1)
    core = lax.axis_index("rep")

    def of_core(a, axis):
        half = a.shape[axis] // 2
        return lax.dynamic_slice_in_dim(a, core * half, half, axis)

    wcat = jnp.stack([
        jnp.concatenate([of_core(w_key, 1), of_core(w_value, 1)], axis=1), of_core(w_query, 1)
    ])
    wo = of_core(w_out, 0).T
    base = lax.axis_index("seq") * rows
    qpos = base + jnp.arange(rows, dtype=jnp.int32)
    half = HEAD_WIDTH // 2
    freq = 10000.0 ** (-(jnp.arange(half, dtype=F32) * 2.0) / HEAD_WIDTH)
    angle = qpos.astype(F32)[:, None] * freq[None, :]
    cosine, sine = jnp.cos(angle), jnp.sin(angle)
    return block(
        tokens.T, gain, wcat, wo,
        query_gain.reshape(1, -1), key_gain.reshape(1, -1),
        jnp.concatenate([cosine, cosine], axis=1), jnp.concatenate([-sine, sine], axis=1),
    ).reshape(width, rows).T


def solution(mesh):
    return jax.shard_map(
        shards,
        mesh=mesh,
        in_specs=(
            P(("rep", "seq"), "hid"),
            P(),
            P("seq", "hid"),
            P("seq", "hid"),
            P("seq", "hid"),
            P(),
            P(),
            P("hid", "seq"),
        ),
        out_specs=P(("rep", "seq"), "hid"),
        check_vma=False,
    )
```

```python
import functools

import jax
import jax.numpy as jnp
from jax import lax
from jax.experimental import pallas as pl
from jax.experimental.pallas import tpu as pltpu
from jax.sharding import PartitionSpec as P

HEAD_WIDTH = 128
WINDOW = 1024
QSCALE = 168
DEPTH = 2
RING = 4
QB = 128
OUT_PARTS = (176, 160)
VMEM_BYTES = 60 * 2**20
MESH = pl.DeviceIdType.MESH
BF16 = jnp.bfloat16
F32 = jnp.float32


def place():
    seq = lax.axis_index("seq")
    return lax.rem(seq, RING), lax.axis_index("hid"), lax.div(seq, RING), lax.axis_index("rep")


def device(x, y, z, r):
    return {"seq": z * RING + x, "hid": y, "rep": r}


def step(a, by):
    return lax.rem(a + by + RING, RING)


def send(src, dst, send_sem, recv_sem, dev):
    copy = pltpu.make_async_remote_copy(
        src_ref=src,
        dst_ref=dst,
        send_sem=send_sem,
        recv_sem=recv_sem,
        device_id=dev,
        device_id_type=MESH,
    )
    copy.start()
    return copy


def greet(devs):
    barrier = pltpu.get_barrier_semaphore()
    for dev in devs:
        pl.semaphore_signal(barrier, inc=1, device_id=dev, device_id_type=MESH)
    return lambda: pl.semaphore_wait(barrier, len(devs))


class Gather:
    def __init__(self, go, src, buf, c1, c2, along1, along2, sibling, sems):
        self.go, self.buf, self.c1, self.c2 = go, buf, c1, c2
        self.along = (along1, along2)
        self.other = sibling
        self.send, self.recv, self.ssend, self.srecv, self.loc = sems
        self.sib = []
        self.own = []
        for i, (part, at, size) in enumerate(src):
            to = self.piece(c2, c1).at[:, pl.ds(at, size)]
            self.own.append(pltpu.make_async_copy(part, to, self.loc.at[i]))
            self.own[i].start()

    def piece(self, c2, c1):
        return self.buf.at[c2 * RING + c1]

    def copy(self, src, dst, i, stage, by):
        return self.go(src, dst, self.send.at[i], self.recv.at[i], self.along[stage](by))

    def to_sibling(self, ref):
        if self.other is None:
            return
        i = len(self.sib)
        self.sib.append(self.go(ref, ref, self.ssend.at[i], self.srecv.at[i], self.other))

    def start(self):
        own = self.piece(self.c2, self.c1)
        for copy in self.own:
            copy.wait()
        self.a = [self.copy(own, own, i, 0, by) for i, by in enumerate((1, -1))]

    def pass_first(self):
        half = self.buf.shape[2] // 2
        self.b = []
        for i, by in enumerate((1, -1)):
            self.a[i].wait_recv()
            ref = self.piece(self.c2, step(self.c1, -by)).at[:, pl.ds(i * half, half)]
            self.b.append(self.copy(ref, ref, 2 + i, 0, by))

    def part(self, row, i):
        return self.buf.at[pl.ds(row * RING + 2 * i, 2)]

    def rows(self):
        for copy in self.b:
            copy.wait_recv()
        self.early, self.late = [], []
        for group, flip in ((self.early, 0), (self.late, 1)):
            for i, by in enumerate((1, -1)):
                ref = self.part(self.c2, i ^ flip)
                group.append(self.copy(ref, ref, 4 + 2 * flip + i, 1, by))
        self.to_sibling(self.buf.at[pl.ds(self.c2 * RING, RING)])

    def pass_rows(self):
        self.f = []
        for i, by in enumerate((1, -1)):
            self.early[i].wait_recv()
            ref = self.part(step(self.c2, -by), i)
            self.f.append(self.copy(ref, ref, 8 + i, 1, by))
            self.to_sibling(ref)

    def rest(self):
        for i, by in enumerate((1, -1)):
            self.late[i].wait_recv()
            self.to_sibling(self.part(step(self.c2, -by), 1 - i))

    def last(self):
        for i in range(2):
            self.f[i].wait_recv()
            self.to_sibling(self.part(step(self.c2, 2), i))

    def done(self):
        for copy in self.sib:
            copy.wait_recv()


def block_kernel(
    tok_ref, gain_ref, wq_ref, wk_ref, wv_ref, wo_ref, qg_ref, kg_ref, cos_ref, sin_ref,
    out_ref,
    tokbuf, wbuf, wo_bufs, xbuf, acc, sums, kvbuf, relay, heads, others, sbuf, rhalf, rfull,
    wsend, wrecv, sib_send, sib_recv, loc, tok_sem,
    ssend, srecv, xsend, xrecv, xssend, xsrecv, hsend, hrecv, osend, orecv, rsend, rrecv,
):
    x, y, z, r = place()
    width, rows = tok_ref.shape
    count = RING * RING
    seq = z * RING + x
    one = 1 - r

    def along1(by):
        return device(step(x, by * one), y, step(z, by * r), r)

    def along2(by):
        return device(step(x, by * r), y, step(z, by * one), r)

    def along_x(by):
        return device(step(x, by), y, z, r)

    def along_y(by):
        return device(x, step(y, by), z, r)

    def along_z(by):
        return device(x, y, step(z, by), r)

    def at_seq(s):
        return {"seq": s, "hid": y, "rep": r}

    def around(s):
        return lax.rem(s + count, count)

    sibling = device(x, y, z, 1 - r)
    after = at_seq(around(seq + 1))
    before = at_seq(around(seq - 1))
    via = device(step(x, -1), y, step(z, lax.div(x + 2, RING)), r)
    back = step(x, 1)
    via_from = device(back, y, step(z, -lax.div(back + 2, RING)), r)
    arrived = greet([along_x(1), along_x(-1), along_z(1), along_z(-1),
                     along_y(1), along_y(-1), along_y(2),
                     sibling, after, before, via, via_from])

    sent = []

    def go(*args):
        copy = send(*args)
        sent.append(copy)
        return copy

    def sems(ph):
        side = max(ph - 2, 0)
        return wsend.at[ph], wrecv.at[ph], sib_send.at[side], sib_recv.at[side], loc.at[ph]

    c1, c2 = x * one + z * r, z * one + x * r
    cols, depth = wbuf.shape[3], wbuf.shape[2]
    half = cols // 2

    def core_cols(size):
        return pl.ds(pl.multiple_of(r * size, size), size)

    tok = tokbuf
    fetch = pltpu.make_async_copy(tok_ref, tok, tok_sem)
    kv = Gather(go, [(wk_ref.at[:, core_cols(half)], 0, half), (wv_ref.at[:, core_cols(half)], half, half)],
                wbuf.at[0], c1, c2, along1, along2, None, sems(0))
    fetch.start()
    qq = Gather(go, [(wq_ref.at[:, core_cols(cols)], 0, cols)],
                wbuf.at[1], c1, c2, along1, along2, None, sems(1))
    outs, starts = [], []
    for n, buf in enumerate(wo_bufs):
        starts.append(sum(b.shape[2] for b in wo_bufs[:n]))
        src = wo_ref.at[pl.ds(starts[n], buf.shape[2]), core_cols(cols)]
        outs.append(Gather(go, [(src, 0, cols)], buf.at[r], c1, c2, along1, along2, sibling,
                           sems(2 + n)))

    fetch.wait()
    raw = tok[...].astype(F32)
    sums[y] = jnp.sum(raw * raw, axis=0, keepdims=True)
    arrived()
    kv.start()
    told = [go(sums.at[y], sums.at[y], ssend.at[i], srecv.at[i], along_y(by))
            for i, by in enumerate((1, 2, 3))]
    for one_of in (qq, *outs):
        one_of.start()
    for one_of in (kv, qq, *outs):
        one_of.pass_first()
    for copy in told:
        copy.wait_recv()
    total = sums[0] + sums[1] + sums[2] + sums[3]
    scale = lax.rsqrt(total * (1.0 / (RING * width)) + 1e-06)

    lanes = 128
    chunk = rows // 2
    part_rows = chunk // 2

    skew = lax.rem(y * width, lanes)

    def rows_of(c):
        return pl.ds(c * chunk, chunk)

    def norm(c):
        mine = scale[:, c * chunk:(c + 1) * chunk]

        def norm_at(at, size):
            part = tok[pl.ds(at, size), rows_of(c)].astype(F32)
            wide = 2 * size if size == lanes else lanes
            seen = gain_ref[:, pl.ds(pl.multiple_of(y * width - skew + at, lanes), wide)]
            gain = jnp.where(skew == 0, seen[:, :size], seen[:, lanes // 2:lanes // 2 + size])
            xbuf[r, y, rows_of(c), pl.ds(at, size)] = ((part * mine).T * gain).astype(BF16)

        def norm_step(i, carry):
            norm_at(pl.multiple_of(i * lanes, lanes), lanes)
            return carry

        lax.fori_loop(0, width // lanes, norm_step, 0)
        if width % lanes:
            norm_at(width // lanes * lanes, width % lanes)

    def x_part(block, i):
        return xbuf.at[r, block, pl.ds(i * part_rows, part_rows)]

    x_early, x_late, x_last, x_sib = {}, {}, {}, {0: [], 1: []}

    def x_over(c, ref):
        i = 7 * c + len(x_sib[c])
        x_sib[c].append(go(ref, ref, xssend.at[i], xsrecv.at[i], sibling))

    def x_send(c):
        for flip, group in enumerate((x_early, x_late)):
            group[c] = []
            for i, by in enumerate((1, -1)):
                ref = x_part(y, 2 * c + (i ^ flip))
                at = 6 * c + 2 * flip + i
                group[c].append(go(ref, ref, xsend.at[at], xrecv.at[at], along_y(by)))
        x_over(c, xbuf.at[r, y, rows_of(c)])

    def x_pass(c):
        x_last[c] = []
        for i, by in enumerate((1, -1)):
            x_early[c][i].wait_recv()
            ref = x_part(step(y, -by), 2 * c + i)
            at = 6 * c + 4 + i
            x_last[c].append(go(ref, ref, xsend.at[at], xrecv.at[at], along_y(by)))
            x_over(c, ref)

    def x_rest(c):
        for i, by in enumerate((1, -1)):
            x_late[c][i].wait_recv()
            x_over(c, x_part(step(y, -by), 2 * c + 1 - i))

    def x_end(c):
        for i in range(2):
            x_last[c][i].wait_recv()
            x_over(c, x_part(step(y, 2), 2 * c + i))

    def slots(kind, t, j):
        low = 1 - kind
        return t * (RING * low + kind) + j * (low + RING * kind)

    def multiply(ph, h, at, first):
        right = jnp.concatenate([wbuf[ph, slots(r, h, j)] for j in range(RING)], axis=0)
        for side in range(2):
            part = jnp.dot(xbuf[side, h, at], right, preferred_element_type=F32)
            if first:
                acc[side, at] = part
            else:
                acc[side, at] += part

    def turn(u, gain, at):
        u = u * lax.rsqrt(jnp.mean(u * u, axis=-1, keepdims=True) + 1e-06) * gain
        cosine, sine = cos_ref[at], sin_ref[at]
        cosine = jnp.concatenate([cosine, cosine], axis=1)
        sine = jnp.concatenate([-sine, sine], axis=1)
        return u * cosine + pltpu.roll(u, HEAD_WIDTH // 2, 1) * sine

    key_gain, query_gain = kg_ref[...], qg_ref[...]
    pair_width = 2 * HEAD_WIDTH

    def block_rows(i, c):
        return pl.ds(i * rows + c * chunk, chunk)

    def keys_values(c):
        at = rows_of(c)

        def of_side(side, carry):
            for head in range(2):
                cols = pl.ds(head * HEAD_WIDTH, HEAD_WIDTH)
                kvbuf[side, block_rows(2, c), cols] = turn(acc[side, at, cols], key_gain, at).astype(BF16)
            cols = pl.ds(pair_width, pair_width)
            kvbuf[side, block_rows(2, c), cols] = acc[side, at, cols].astype(BF16)
            return carry

        lax.fori_loop(0, 2, of_side, 0)

    halo = {}

    def halo_go(c, i, src, dst, dev):
        halo[c, i] = go(src, dst, hsend.at[5 * c + i], hrecv.at[5 * c + i], dev)

    def halo_send(c):
        own0, own1 = (kvbuf.at[side, block_rows(2, c)] for side in range(2))
        halo_go(c, 0, own0, kvbuf.at[0, block_rows(1, c)], after)
        halo_go(c, 2, own1, relay.at[c], via)
        halo_go(c, 1, own1, kvbuf.at[1, block_rows(1, c)], after)

    def halo_pass(c):
        halo[c, 0].wait_recv()
        halo_go(c, 3, kvbuf.at[0, block_rows(1, c)], kvbuf.at[0, block_rows(0, c)], after)
        halo[c, 2].wait_recv()
        halo_go(c, 4, relay.at[c], kvbuf.at[1, block_rows(0, c)], along_x(-1))

    norm(1)
    x_send(1)
    kv.rows()
    norm(0)
    x_pass(1)
    x_send(0)
    kv.pass_rows()
    qq.rows()
    x_rest(1)
    kv.rest()
    x_end(1)
    kv.last()
    for copy in x_sib[1]:
        copy.wait_recv()
    multiply(0, y, rows_of(1), True)
    lax.fori_loop(1, RING, lambda i, c: (multiply(0, step(y, i), rows_of(1), False), c)[1], 0)
    keys_values(1)
    halo_send(1)
    x_pass(0)
    qq.pass_rows()
    x_rest(0)
    for copy in x_sib[0]:
        copy.wait_recv()
    multiply(0, y, rows_of(0), True)
    halo_pass(1)
    lax.fori_loop(0, 2, lambda i, c: (multiply(0, step(y, 1 + 2 * i), rows_of(0), False), c)[1], 0)
    x_end(0)
    for copy in x_sib[0][5:]:
        copy.wait_recv()
    multiply(0, step(y, 2), rows_of(0), False)
    keys_values(0)
    halo_send(0)
    qq.rest()
    qq.last()
    whole = pl.ds(0, rows)
    multiply(1, y, whole, True)
    lax.fori_loop(1, RING, lambda i, c: (multiply(1, step(y, i), whole, False), c)[1], 0)

    def queries(side, carry):
        for head in range(4):
            cols = pl.ds(head * HEAD_WIDTH, HEAD_WIDTH)
            turned = turn(acc[side, :, cols], query_gain, whole) * QSCALE ** (-0.5)
            heads[side, :, cols] = turned.astype(BF16)
        return carry

    lax.fori_loop(0, 2, queries, 0)
    halo_pass(0)
    outs[0].rows()
    for c in (1, 0):
        for i in (1, 3, 4):
            halo[c, i].wait_recv()

    span = WINDOW + QB
    ri = lax.broadcasted_iota(jnp.int32, (QB, QB), 0)
    ci = lax.broadcasted_iota(jnp.int32, (QB, QB), 1)
    recent = jnp.concatenate([ci <= ri] * 2, axis=0)
    oldest = jnp.concatenate([ci > ri] * 2, axis=0)
    lane = lax.broadcasted_iota(jnp.int32, (1, span), 1)

    def attend(side, it):
        g = lax.rem(it, 2)
        i = lax.div(it, 2)
        at = pl.multiple_of(i * QB, QB)
        k_cols = pl.ds(pl.multiple_of(g * HEAD_WIDTH, HEAD_WIDTH), HEAD_WIDTH)
        v_cols = pl.ds(pl.multiple_of((2 + g) * HEAD_WIDTH, HEAD_WIDTH), HEAD_WIDTH)
        pair = [pl.ds(pl.multiple_of((2 * g + j) * HEAD_WIDTH, HEAD_WIDTH), HEAD_WIDTH)
                for j in range(2)]
        q = jnp.concatenate([heads[side, pl.ds(at, QB), c] for c in pair], axis=0)
        k = kvbuf[side, pl.ds(at, span), k_cols]
        v = kvbuf[side, pl.ds(at, span), v_cols]
        s = lax.dot_general(q, k, (((1,), (1,)), ((), ())), preferred_element_type=F32)
        present = lane + at >= DEPTH * rows - seq * rows
        s = jnp.concatenate([
            jnp.where(oldest, s[:, :QB], -jnp.inf), s[:, QB:WINDOW],
            jnp.where(recent, s[:, WINDOW:], -jnp.inf)], axis=1)
        s = jnp.where(present, s, -jnp.inf)
        p = jnp.exp(s - jnp.max(s, axis=1, keepdims=True))
        p = (p * (1.0 / jnp.sum(p, axis=1, keepdims=True))).astype(BF16)
        o = jnp.dot(p, v, preferred_element_type=F32).astype(BF16)
        for j in range(2):
            heads[side, pl.ds(at, QB), pair[j]] = o[j * QB:(j + 1) * QB]

    def attend_all(side):
        lax.fori_loop(0, 2 * (rows // QB), lambda it, c: (attend(side, it), c)[1], 0)

    attend_all(1 - r)
    swap = go(heads.at[1 - r], others, osend, orecv, sibling)
    outs[0].pass_rows()
    outs[1].rows()
    attend_all(r)
    outs[0].rest()
    outs[0].last()
    swap.wait_recv()

    near, far = pl.ds(0, chunk), pl.ds(chunk, chunk)
    flows = {}

    def terms(n, t, dest):
        buf = wo_bufs[n]
        start, size = starts[n], buf.shape[2]

        def one_piece(j, carry):
            part = lax.dot_general(buf[r, slots(r, t, j)], heads[r], (((1,), (1,)), ((), ())),
                                   preferred_element_type=F32)
            part += lax.dot_general(buf[1 - r, slots(1 - r, t, j)], others[...],
                                    (((1,), (1,)), ((), ())), preferred_element_type=F32)
            dest[j, pl.ds(start, size), :] = part.astype(BF16)
            return carry

        lax.fori_loop(0, RING, one_piece, 0)

    def cut(n):
        return pl.ds(starts[n], wo_bufs[n].shape[2])

    def flow(n, i, src, dst, by):
        flows[n, i] = go(src, dst, rsend.at[6 * n + i], rrecv.at[6 * n + i], along_y(by))

    def spread(n):
        at = cut(n)
        terms(n, step(y, 2), sbuf.at[0])
        flow(n, 0, sbuf.at[0, :, at, near], rhalf.at[0, :, at], 1)
        flow(n, 1, sbuf.at[0, :, at, far], rhalf.at[1, :, at], -1)
        terms(n, step(y, 1), sbuf.at[1])
        flow(n, 2, sbuf.at[1, :, at, far], rfull.at[0, :, at, far], 1)
        terms(n, step(y, -1), sbuf.at[2])
        flow(n, 3, sbuf.at[2, :, at, near], rfull.at[1, :, at, near], -1)

    def add(n):
        at = cut(n)
        for i, half, by in ((0, near, 1), (1, far, -1)):
            flows[n, i].wait_recv()
            both = sbuf[1 + i, :, at, half].astype(F32) + rhalf[i, :, at].astype(F32)
            sbuf[1 + i, :, at, half] = both.astype(BF16)
            flow(n, 4 + i, sbuf.at[1 + i, :, at, half], rfull.at[i, :, at, half], by)

    def close(n):
        at = cut(n)
        for i in range(2, 6):
            flows[n, i].wait_recv()
        out_ref[:, at, :] = (out_ref[:, at, :].astype(F32) + rfull[0, :, at, :].astype(F32)
                             + rfull[1, :, at, :].astype(F32)).astype(BF16)

    for n in range(len(outs)):
        outs[n].done()
        spread(n)
        if n + 1 < len(outs):
            outs[n + 1].pass_rows()
        if n + 2 < len(outs):
            outs[n + 2].rows()
        terms(n, y, out_ref)
        add(n)
        if n + 1 < len(outs):
            outs[n + 1].rest()
            outs[n + 1].last()
    for n in range(len(outs)):
        close(n)
    for copy in sent:
        copy.wait_send()


def block(tok, gain, wq, wk, wv, wo, query_gain, key_gain, cosine, sine):
    width, rows = tok.shape
    depth, cols = wk.shape
    parts = len(OUT_PARTS)
    dma = pltpu.SemaphoreType.DMA
    vmem = pl.BlockSpec(memory_space=pltpu.VMEM)
    hbm = pl.BlockSpec(memory_space=pl.ANY)
    return pl.pallas_call(
        block_kernel,
        out_shape=jax.ShapeDtypeStruct((RING, depth, rows), BF16),
        in_specs=[hbm, vmem, hbm, hbm, hbm, hbm, vmem, vmem, vmem, vmem],
        out_specs=vmem,
        scratch_shapes=[
            pltpu.VMEM((width, rows), BF16),
            pltpu.VMEM((2, RING * RING, depth, cols), BF16),
            [pltpu.VMEM((2, RING * RING, size, cols), BF16) for size in OUT_PARTS],
            pltpu.VMEM((2, RING, rows, width), BF16),
            pltpu.VMEM((2, rows, cols), F32),
            pltpu.VMEM((RING, 1, rows), F32),
            pltpu.VMEM((2, 3 * rows, cols), BF16),
            pltpu.VMEM((2, rows // 2, cols), BF16),
            pltpu.VMEM((2, rows, cols), BF16),
            pltpu.VMEM((rows, cols), BF16),
            pltpu.VMEM((3, RING, depth, rows), BF16),
            pltpu.VMEM((2, RING, depth, rows // 2), BF16),
            pltpu.VMEM((2, RING, depth, rows), BF16),
            dma((2 + parts, 10)), dma((2 + parts, 10)), dma((parts, 7)), dma((parts, 7)),
            dma((2 + parts, 2)), dma,
            dma((3,)), dma((3,)), dma((12,)), dma((12,)), dma((14,)), dma((14,)),
            dma((10,)), dma((10,)), dma, dma, dma((6 * parts,)), dma((6 * parts,)),
        ],
        compiler_params=pltpu.CompilerParams(
            collective_id=0, has_side_effects=True, vmem_limit_bytes=VMEM_BYTES
        ),
    )(tok, gain, wq, wk, wv, wo, query_gain, key_gain, cosine, sine)


def shards(tokens, norm_gain, w_query, w_key, w_value, query_gain, key_gain, w_out):
    rows, width = tokens.shape
    base = lax.axis_index("seq") * rows
    qpos = base + jnp.arange(rows, dtype=jnp.int32)
    half = HEAD_WIDTH // 2
    freq = 10000.0 ** (-(jnp.arange(half, dtype=F32) * 2.0) / HEAD_WIDTH)
    angle = qpos.astype(F32)[:, None] * freq[None, :]
    cosine, sine = jnp.cos(angle), jnp.sin(angle)
    return block(
        tokens.T, norm_gain.reshape(1, -1), w_query, w_key, w_value, w_out.T,
        query_gain.reshape(1, -1), key_gain.reshape(1, -1), cosine, sine,
    ).reshape(width, rows).T


def solution(mesh):
    return jax.shard_map(
        shards,
        mesh=mesh,
        in_specs=(
            P(("rep", "seq"), "hid"),
            P(),
            P("seq", "hid"),
            P("seq", "hid"),
            P("seq", "hid"),
            P(),
            P(),
            P("hid", "seq"),
        ),
        out_specs=P(("rep", "seq"), "hid"),
        check_vma=False,
    )
```

```python
import functools

import jax
import jax.numpy as jnp
from jax import lax
from jax.experimental import pallas as pl
from jax.experimental.pallas import tpu as pltpu
from jax.sharding import PartitionSpec as P

HEAD_WIDTH = 128
WINDOW = 1024
QSCALE = 168
DEPTH = 2
RING = 4
QB = 128
OUT_PARTS = (144, 192)
VMEM_BYTES = 60 * 2**20
MESH = pl.DeviceIdType.MESH
BF16 = jnp.bfloat16
F32 = jnp.float32


def place():
    seq = lax.axis_index("seq")
    return lax.rem(seq, RING), lax.axis_index("hid"), lax.div(seq, RING), lax.axis_index("rep")


def device(x, y, z, r):
    return {"seq": z * RING + x, "hid": y, "rep": r}


def step(a, by):
    return lax.rem(a + by + RING, RING)


def send(src, dst, send_sem, recv_sem, dev):
    copy = pltpu.make_async_remote_copy(
        src_ref=src,
        dst_ref=dst,
        send_sem=send_sem,
        recv_sem=recv_sem,
        device_id=dev,
        device_id_type=MESH,
    )
    copy.start()
    return copy


def greet(devs):
    barrier = pltpu.get_barrier_semaphore()
    for dev in devs:
        pl.semaphore_signal(barrier, inc=1, device_id=dev, device_id_type=MESH)
    return lambda: pl.semaphore_wait(barrier, len(devs))


class Gather:
    def __init__(self, go, src, buf, c1, c2, along1, along2, sibling, sems):
        self.go, self.buf, self.c1, self.c2 = go, buf, c1, c2
        self.along = (along1, along2)
        self.other = sibling
        self.send, self.recv, self.ssend, self.srecv, self.loc = sems
        self.sib = []
        self.low = 2
        self.own = []
        for i, (part, at, size) in enumerate(src):
            to = self.piece(c2, c1).at[:, pl.ds(at, size)]
            self.own.append(pltpu.make_async_copy(part, to, self.loc.at[i]))
            self.own[i].start()

    def piece(self, c2, c1):
        return self.buf.at[c2 * RING + c1]

    def copy(self, src, dst, i, stage, by):
        return self.go(src, dst, self.send.at[i], self.recv.at[i], self.along[stage](by))

    def to_sibling(self, ref):
        if self.other is None:
            return
        i = len(self.sib)
        self.sib.append(self.go(ref, ref, self.ssend.at[i], self.srecv.at[i], self.other))

    def start(self):
        own = self.piece(self.c2, self.c1)
        for copy in self.own:
            copy.wait()
        self.a = [self.copy(own, own, i, 0, by) for i, by in enumerate((1, -1))]

    def pass_first(self):
        half = self.buf.shape[2] // 2
        self.b = []
        for i, by in enumerate((1, -1)):
            self.a[i].wait_recv()
            ref = self.piece(self.c2, step(self.c1, -by)).at[:, pl.ds(i * half, half)]
            self.b.append(self.copy(ref, ref, 2 + i, 0, by))

    def part(self, row, i):
        return self.buf.at[pl.ds(row * RING + self.low * i, RING - self.low if i else self.low)]

    def rows(self):
        for copy in self.b:
            copy.wait_recv()
        self.early, self.late = [], []
        for group, flip in ((self.early, 0), (self.late, 1)):
            for i, by in enumerate((1, -1)):
                ref = self.part(self.c2, i ^ flip)
                group.append(self.copy(ref, ref, 4 + 2 * flip + i, 1, by))
        self.to_sibling(self.buf.at[pl.ds(self.c2 * RING, RING)])

    def pass_rows(self):
        self.f = []
        for i, by in enumerate((1, -1)):
            self.early[i].wait_recv()
            ref = self.part(step(self.c2, -by), i)
            self.f.append(self.copy(ref, ref, 8 + i, 1, by))
            self.to_sibling(ref)

    def rest(self):
        for i, by in enumerate((1, -1)):
            self.late[i].wait_recv()
            self.to_sibling(self.part(step(self.c2, -by), 1 - i))

    def last(self):
        for i in range(2):
            self.f[i].wait_recv()
            self.to_sibling(self.part(step(self.c2, 2), i))

    def done(self):
        for copy in self.sib:
            copy.wait_recv()


def block_kernel(
    tok_ref, gain_ref, wq_ref, wk_ref, wv_ref, wo_ref, qg_ref, kg_ref, cos_ref, sin_ref,
    out_ref,
    tokbuf, wbuf, wo_bufs, xbuf, acc, sums, kvbuf, relay, heads, others, sbuf, rhalf, rfull,
    wsend, wrecv, sib_send, sib_recv, loc, tok_sem,
    ssend, srecv, xsend, xrecv, xssend, xsrecv, hsend, hrecv, osend, orecv, rsend, rrecv,
):
    x, y, z, r = place()
    width, rows = tok_ref.shape
    count = RING * RING
    seq = z * RING + x
    one = 1 - r

    def along1(by):
        return device(step(x, by * one), y, step(z, by * r), r)

    def along2(by):
        return device(step(x, by * r), y, step(z, by * one), r)

    def along_x(by):
        return device(step(x, by), y, z, r)

    def along_y(by):
        return device(x, step(y, by), z, r)

    def along_z(by):
        return device(x, y, step(z, by), r)

    def at_seq(s):
        return {"seq": s, "hid": y, "rep": r}

    def around(s):
        return lax.rem(s + count, count)

    sibling = device(x, y, z, 1 - r)
    after = at_seq(around(seq + 1))
    before = at_seq(around(seq - 1))
    via = device(step(x, -1), y, step(z, lax.div(x + 2, RING)), r)
    back = step(x, 1)
    via_from = device(back, y, step(z, -lax.div(back + 2, RING)), r)
    arrived = greet([along_x(1), along_x(-1), along_z(1), along_z(-1),
                     along_y(1), along_y(-1), along_y(2),
                     sibling, after, before, via, via_from])

    sent = []

    def go(*args):
        copy = send(*args)
        sent.append(copy)
        return copy

    def sems(ph):
        side = max(ph - 2, 0)
        return wsend.at[ph], wrecv.at[ph], sib_send.at[side], sib_recv.at[side], loc.at[ph]

    c1, c2 = x * one + z * r, z * one + x * r
    cols, depth = wbuf.shape[3], wbuf.shape[2]
    half = cols // 2

    def core_cols(size):
        return pl.ds(pl.multiple_of(r * size, size), size)

    tok = tokbuf
    fetch = pltpu.make_async_copy(tok_ref, tok, tok_sem)
    kv = Gather(go, [(wk_ref.at[:, core_cols(half)], 0, half), (wv_ref.at[:, core_cols(half)], half, half)],
                wbuf.at[0], c1, c2, along1, along2, None, sems(0))
    fetch.start()
    qq = Gather(go, [(wq_ref.at[:, core_cols(cols)], 0, cols)],
                wbuf.at[1], c1, c2, along1, along2, None, sems(1))
    qq.low = 1
    outs, starts = [], []
    for n, buf in enumerate(wo_bufs):
        starts.append(sum(b.shape[2] for b in wo_bufs[:n]))
        src = wo_ref.at[pl.ds(starts[n], buf.shape[2]), core_cols(cols)]
        outs.append(Gather(go, [(src, 0, cols)], buf.at[r], c1, c2, along1, along2, sibling,
                           sems(2 + n)))

    fetch.wait()
    raw = tok[...].astype(F32)
    sums[y] = jnp.sum(raw * raw, axis=0, keepdims=True)
    arrived()
    kv.start()
    told = [go(sums.at[y], sums.at[y], ssend.at[i], srecv.at[i], along_y(by))
            for i, by in enumerate((1, 2, 3))]
    for one_of in (qq, *outs):
        one_of.start()
    for one_of in (kv, qq, *outs):
        one_of.pass_first()
    for copy in told:
        copy.wait_recv()
    total = sums[0] + sums[1] + sums[2] + sums[3]
    scale = lax.rsqrt(total * (1.0 / (RING * width)) + 1e-06)

    lanes = 128
    chunk = rows // 2
    part_rows = chunk // 2

    skew = lax.rem(y * width, lanes)

    def rows_of(c):
        return pl.ds(c * chunk, chunk)

    def norm(c):
        mine = scale[:, c * chunk:(c + 1) * chunk]

        def norm_at(at, size):
            part = tok[pl.ds(at, size), rows_of(c)].astype(F32)
            wide = 2 * size if size == lanes else lanes
            seen = gain_ref[:, pl.ds(pl.multiple_of(y * width - skew + at, lanes), wide)]
            gain = jnp.where(skew == 0, seen[:, :size], seen[:, lanes // 2:lanes // 2 + size])
            xbuf[r, y, rows_of(c), pl.ds(at, size)] = ((part * mine).T * gain).astype(BF16)

        def norm_step(i, carry):
            norm_at(pl.multiple_of(i * lanes, lanes), lanes)
            return carry

        lax.fori_loop(0, width // lanes, norm_step, 0)
        if width % lanes:
            norm_at(width // lanes * lanes, width % lanes)

    def x_part(block, i):
        return xbuf.at[r, block, pl.ds(i * part_rows, part_rows)]

    x_early, x_late, x_last, x_sib = {}, {}, {}, {0: [], 1: []}

    def x_over(c, ref):
        i = 7 * c + len(x_sib[c])
        x_sib[c].append(go(ref, ref, xssend.at[i], xsrecv.at[i], sibling))

    def x_send(c):
        for flip, group in enumerate((x_early, x_late)):
            group[c] = []
            for i, by in enumerate((1, -1)):
                ref = x_part(y, 2 * c + (i ^ flip))
                at = 6 * c + 2 * flip + i
                group[c].append(go(ref, ref, xsend.at[at], xrecv.at[at], along_y(by)))
        x_over(c, xbuf.at[r, y, rows_of(c)])

    def x_pass(c):
        x_last[c] = []
        for i, by in enumerate((1, -1)):
            x_early[c][i].wait_recv()
            ref = x_part(step(y, -by), 2 * c + i)
            at = 6 * c + 4 + i
            x_last[c].append(go(ref, ref, xsend.at[at], xrecv.at[at], along_y(by)))
            x_over(c, ref)

    def x_rest(c):
        for i, by in enumerate((1, -1)):
            x_late[c][i].wait_recv()
            x_over(c, x_part(step(y, -by), 2 * c + 1 - i))

    def x_end(c):
        for i in range(2):
            x_last[c][i].wait_recv()
            x_over(c, x_part(step(y, 2), 2 * c + i))

    def slots(kind, t, j):
        low = 1 - kind
        return t * (RING * low + kind) + j * (low + RING * kind)

    def multiply(ph, h, at, first):
        right = jnp.concatenate([wbuf[ph, slots(r, h, j)] for j in range(RING)], axis=0)
        for side in range(2):
            part = jnp.dot(xbuf[side, h, at], right, preferred_element_type=F32)
            if first:
                acc[side, at] = part
            else:
                acc[side, at] += part

    def turn(u, gain, at):
        u = u * lax.rsqrt(jnp.mean(u * u, axis=-1, keepdims=True) + 1e-06) * gain
        cosine, sine = cos_ref[at], sin_ref[at]
        cosine = jnp.concatenate([cosine, cosine], axis=1)
        sine = jnp.concatenate([-sine, sine], axis=1)
        return u * cosine + pltpu.roll(u, HEAD_WIDTH // 2, 1) * sine

    key_gain, query_gain = kg_ref[...], qg_ref[...]
    pair_width = 2 * HEAD_WIDTH

    def block_rows(i, c):
        return pl.ds(i * rows + c * chunk, chunk)

    def keys_values(c):
        at = rows_of(c)

        def of_side(side, carry):
            for head in range(2):
                cols = pl.ds(head * HEAD_WIDTH, HEAD_WIDTH)
                kvbuf[side, block_rows(2, c), cols] = turn(acc[side, at, cols], key_gain, at).astype(BF16)
            cols = pl.ds(pair_width, pair_width)
            kvbuf[side, block_rows(2, c), cols] = acc[side, at, cols].astype(BF16)
            return carry

        lax.fori_loop(0, 2, of_side, 0)

    halo = {}

    def halo_go(c, i, src, dst, dev):
        halo[c, i] = go(src, dst, hsend.at[5 * c + i], hrecv.at[5 * c + i], dev)

    def halo_send(c):
        own0, own1 = (kvbuf.at[side, block_rows(2, c)] for side in range(2))
        halo_go(c, 0, own0, kvbuf.at[0, block_rows(1, c)], after)
        halo_go(c, 2, own1, relay.at[c], via)
        halo_go(c, 1, own1, kvbuf.at[1, block_rows(1, c)], after)

    def halo_pass(c):
        halo[c, 0].wait_recv()
        halo_go(c, 3, kvbuf.at[0, block_rows(1, c)], kvbuf.at[0, block_rows(0, c)], after)
        halo[c, 2].wait_recv()
        halo_go(c, 4, relay.at[c], kvbuf.at[1, block_rows(0, c)], along_x(-1))

    norm(1)
    x_send(1)
    kv.rows()
    norm(0)
    x_pass(1)
    x_send(0)
    kv.pass_rows()
    qq.rows()
    x_rest(1)
    kv.rest()
    x_end(1)
    kv.last()
    for copy in x_sib[1]:
        copy.wait_recv()
    multiply(0, y, rows_of(1), True)
    lax.fori_loop(1, RING, lambda i, c: (multiply(0, step(y, i), rows_of(1), False), c)[1], 0)
    keys_values(1)
    halo_send(1)
    x_pass(0)
    qq.pass_rows()
    x_rest(0)
    for copy in x_sib[0]:
        copy.wait_recv()
    multiply(0, y, rows_of(0), True)
    halo_pass(1)
    lax.fori_loop(0, 2, lambda i, c: (multiply(0, step(y, 1 + 2 * i), rows_of(0), False), c)[1], 0)
    x_end(0)
    for copy in x_sib[0][5:]:
        copy.wait_recv()
    multiply(0, step(y, 2), rows_of(0), False)
    keys_values(0)
    halo_send(0)
    qq.rest()
    qq.last()
    whole = pl.ds(0, rows)
    multiply(1, y, whole, True)
    lax.fori_loop(1, RING, lambda i, c: (multiply(1, step(y, i), whole, False), c)[1], 0)

    def queries(side, carry):
        for head in range(4):
            cols = pl.ds(head * HEAD_WIDTH, HEAD_WIDTH)
            turned = turn(acc[side, :, cols], query_gain, whole) * QSCALE ** (-0.5)
            heads[side, :, cols] = turned.astype(BF16)
        return carry

    lax.fori_loop(0, 2, queries, 0)
    halo_pass(0)
    outs[0].rows()
    for c in (1, 0):
        for i in (1, 3, 4):
            halo[c, i].wait_recv()

    span = WINDOW + QB
    ri = lax.broadcasted_iota(jnp.int32, (QB, QB), 0)
    ci = lax.broadcasted_iota(jnp.int32, (QB, QB), 1)
    recent = jnp.concatenate([ci <= ri] * 2, axis=0)
    oldest = jnp.concatenate([ci > ri] * 2, axis=0)
    lane = lax.broadcasted_iota(jnp.int32, (1, span), 1)

    def attend(side, it):
        g = lax.rem(it, 2)
        i = lax.div(it, 2)
        at = pl.multiple_of(i * QB, QB)
        k_cols = pl.ds(pl.multiple_of(g * HEAD_WIDTH, HEAD_WIDTH), HEAD_WIDTH)
        v_cols = pl.ds(pl.multiple_of((2 + g) * HEAD_WIDTH, HEAD_WIDTH), HEAD_WIDTH)
        pair = [pl.ds(pl.multiple_of((2 * g + j) * HEAD_WIDTH, HEAD_WIDTH), HEAD_WIDTH)
                for j in range(2)]
        q = jnp.concatenate([heads[side, pl.ds(at, QB), c] for c in pair], axis=0)
        k = kvbuf[side, pl.ds(at, span), k_cols]
        v = kvbuf[side, pl.ds(at, span), v_cols]
        s = lax.dot_general(q, k, (((1,), (1,)), ((), ())), preferred_element_type=F32)
        present = lane + at >= DEPTH * rows - seq * rows
        s = jnp.concatenate([
            jnp.where(oldest, s[:, :QB], -jnp.inf), s[:, QB:WINDOW],
            jnp.where(recent, s[:, WINDOW:], -jnp.inf)], axis=1)
        s = jnp.where(present, s, -jnp.inf)
        p = jnp.exp(s - jnp.max(s, axis=1, keepdims=True))
        p = (p * (1.0 / jnp.sum(p, axis=1, keepdims=True))).astype(BF16)
        o = jnp.dot(p, v, preferred_element_type=F32).astype(BF16)
        for j in range(2):
            heads[side, pl.ds(at, QB), pair[j]] = o[j * QB:(j + 1) * QB]

    def attend_all(side):
        lax.fori_loop(0, 2 * (rows // QB), lambda it, c: (attend(side, it), c)[1], 0)

    attend_all(1 - r)
    swap = go(heads.at[1 - r], others, osend, orecv, sibling)
    outs[0].pass_rows()
    outs[1].rows()
    attend_all(r)
    outs[0].rest()
    outs[0].last()
    swap.wait_recv()

    near, far = pl.ds(0, chunk), pl.ds(chunk, chunk)
    flows = {}

    def terms(n, t, dest):
        buf = wo_bufs[n]
        start, size = starts[n], buf.shape[2]

        def one_piece(j, carry):
            part = lax.dot_general(buf[r, slots(r, t, j)], heads[r], (((1,), (1,)), ((), ())),
                                   preferred_element_type=F32)
            part += lax.dot_general(buf[1 - r, slots(1 - r, t, j)], others[...],
                                    (((1,), (1,)), ((), ())), preferred_element_type=F32)
            dest[j, pl.ds(start, size), :] = part.astype(BF16)
            return carry

        lax.fori_loop(0, RING, one_piece, 0)

    def cut(n):
        return pl.ds(starts[n], wo_bufs[n].shape[2])

    def flow(n, i, src, dst, by):
        flows[n, i] = go(src, dst, rsend.at[6 * n + i], rrecv.at[6 * n + i], along_y(by))

    def spread(n):
        at = cut(n)
        terms(n, step(y, 2), sbuf.at[0])
        flow(n, 0, sbuf.at[0, :, at, near], rhalf.at[0, :, at], 1)
        flow(n, 1, sbuf.at[0, :, at, far], rhalf.at[1, :, at], -1)
        terms(n, step(y, 1), sbuf.at[1])
        flow(n, 2, sbuf.at[1, :, at, far], rfull.at[0, :, at, far], 1)
        terms(n, step(y, -1), sbuf.at[2])
        flow(n, 3, sbuf.at[2, :, at, near], rfull.at[1, :, at, near], -1)

    def add(n):
        at = cut(n)
        for i, half, by in ((0, near, 1), (1, far, -1)):
            flows[n, i].wait_recv()
            both = sbuf[1 + i, :, at, half].astype(F32) + rhalf[i, :, at].astype(F32)
            sbuf[1 + i, :, at, half] = both.astype(BF16)
            flow(n, 4 + i, sbuf.at[1 + i, :, at, half], rfull.at[i, :, at, half], by)

    def close(n):
        at = cut(n)
        for i in range(2, 6):
            flows[n, i].wait_recv()
        out_ref[:, at, :] = (out_ref[:, at, :].astype(F32) + rfull[0, :, at, :].astype(F32)
                             + rfull[1, :, at, :].astype(F32)).astype(BF16)

    for n in range(len(outs)):
        outs[n].done()
        spread(n)
        if n + 1 < len(outs):
            outs[n + 1].pass_rows()
        if n + 2 < len(outs):
            outs[n + 2].rows()
        terms(n, y, out_ref)
        add(n)
        if n + 1 < len(outs):
            outs[n + 1].rest()
            outs[n + 1].last()
    for n in range(len(outs)):
        close(n)
    for copy in sent:
        copy.wait_send()


def block(tok, gain, wq, wk, wv, wo, query_gain, key_gain, cosine, sine):
    width, rows = tok.shape
    depth, cols = wk.shape
    parts = len(OUT_PARTS)
    dma = pltpu.SemaphoreType.DMA
    vmem = pl.BlockSpec(memory_space=pltpu.VMEM)
    hbm = pl.BlockSpec(memory_space=pl.ANY)
    return pl.pallas_call(
        block_kernel,
        out_shape=jax.ShapeDtypeStruct((RING, depth, rows), BF16),
        in_specs=[hbm, vmem, hbm, hbm, hbm, hbm, vmem, vmem, vmem, vmem],
        out_specs=vmem,
        scratch_shapes=[
            pltpu.VMEM((width, rows), BF16),
            pltpu.VMEM((2, RING * RING, depth, cols), BF16),
            [pltpu.VMEM((2, RING * RING, size, cols), BF16) for size in OUT_PARTS],
            pltpu.VMEM((2, RING, rows, width), BF16),
            pltpu.VMEM((2, rows, cols), F32),
            pltpu.VMEM((RING, 1, rows), F32),
            pltpu.VMEM((2, 3 * rows, cols), BF16),
            pltpu.VMEM((2, rows // 2, cols), BF16),
            pltpu.VMEM((2, rows, cols), BF16),
            pltpu.VMEM((rows, cols), BF16),
            pltpu.VMEM((3, RING, depth, rows), BF16),
            pltpu.VMEM((2, RING, depth, rows // 2), BF16),
            pltpu.VMEM((2, RING, depth, rows), BF16),
            dma((2 + parts, 10)), dma((2 + parts, 10)), dma((parts, 7)), dma((parts, 7)),
            dma((2 + parts, 2)), dma,
            dma((3,)), dma((3,)), dma((12,)), dma((12,)), dma((14,)), dma((14,)),
            dma((10,)), dma((10,)), dma, dma, dma((6 * parts,)), dma((6 * parts,)),
        ],
        compiler_params=pltpu.CompilerParams(
            collective_id=0, has_side_effects=True, vmem_limit_bytes=VMEM_BYTES
        ),
    )(tok, gain, wq, wk, wv, wo, query_gain, key_gain, cosine, sine)


def shards(tokens, norm_gain, w_query, w_key, w_value, query_gain, key_gain, w_out):
    rows, width = tokens.shape
    base = lax.axis_index("seq") * rows
    qpos = base + jnp.arange(rows, dtype=jnp.int32)
    half = HEAD_WIDTH // 2
    freq = 10000.0 ** (-(jnp.arange(half, dtype=F32) * 2.0) / HEAD_WIDTH)
    angle = qpos.astype(F32)[:, None] * freq[None, :]
    cosine, sine = jnp.cos(angle), jnp.sin(angle)
    return block(
        tokens.T, norm_gain.reshape(1, -1), w_query, w_key, w_value, w_out.T,
        query_gain.reshape(1, -1), key_gain.reshape(1, -1), cosine, sine,
    ).reshape(width, rows).T


def solution(mesh):
    return jax.shard_map(
        shards,
        mesh=mesh,
        in_specs=(
            P(("rep", "seq"), "hid"),
            P(),
            P("seq", "hid"),
            P("seq", "hid"),
            P("seq", "hid"),
            P(),
            P(),
            P("hid", "seq"),
        ),
        out_specs=P(("rep", "seq"), "hid"),
        check_vma=False,
    )
```

```python
import functools

import jax
import jax.numpy as jnp
from jax import lax
from jax.experimental import pallas as pl
from jax.experimental.pallas import tpu as pltpu
from jax.sharding import PartitionSpec as P

HEAD_WIDTH = 128
WINDOW = 1024
QSCALE = 168
DEPTH = 2
RING = 4
QB = 128
OUT_PARTS = (144, 192)
VMEM_BYTES = 60 * 2**20
MESH = pl.DeviceIdType.MESH
BF16 = jnp.bfloat16
F32 = jnp.float32


def place():
    seq = lax.axis_index("seq")
    return lax.rem(seq, RING), lax.axis_index("hid"), lax.div(seq, RING), lax.axis_index("rep")


def device(x, y, z, r):
    return {"seq": z * RING + x, "hid": y, "rep": r}


def step(a, by):
    return lax.rem(a + by + RING, RING)


def send(src, dst, send_sem, recv_sem, dev):
    copy = pltpu.make_async_remote_copy(
        src_ref=src,
        dst_ref=dst,
        send_sem=send_sem,
        recv_sem=recv_sem,
        device_id=dev,
        device_id_type=MESH,
    )
    copy.start()
    return copy


def greet(devs):
    barrier = pltpu.get_barrier_semaphore()
    for dev in devs:
        pl.semaphore_signal(barrier, inc=1, device_id=dev, device_id_type=MESH)
    return lambda: pl.semaphore_wait(barrier, len(devs))


class Gather:
    def __init__(self, go, src, buf, c1, c2, along1, along2, sibling, sems):
        self.go, self.buf, self.c1, self.c2 = go, buf, c1, c2
        self.along = (along1, along2)
        self.other = sibling
        self.send, self.recv, self.ssend, self.srecv, self.loc = sems
        self.sib = []
        self.low = 2
        self.own = []
        for i, (part, at, size) in enumerate(src):
            to = self.piece(c2, c1).at[:, pl.ds(at, size)]
            self.own.append(pltpu.make_async_copy(part, to, self.loc.at[i]))
            self.own[i].start()

    def piece(self, c2, c1):
        return self.buf.at[c2 * RING + c1]

    def copy(self, src, dst, i, stage, by):
        return self.go(src, dst, self.send.at[i], self.recv.at[i], self.along[stage](by))

    def to_sibling(self, ref):
        if self.other is None:
            return
        i = len(self.sib)
        self.sib.append(self.go(ref, ref, self.ssend.at[i], self.srecv.at[i], self.other))

    def start(self):
        own = self.piece(self.c2, self.c1)
        for copy in self.own:
            copy.wait()
        self.a = [self.copy(own, own, i, 0, by) for i, by in enumerate((1, -1))]

    def pass_first(self):
        half = self.buf.shape[2] // 2
        self.b = []
        for i, by in enumerate((1, -1)):
            self.a[i].wait_recv()
            ref = self.piece(self.c2, step(self.c1, -by)).at[:, pl.ds(i * half, half)]
            self.b.append(self.copy(ref, ref, 2 + i, 0, by))

    def part(self, row, i):
        return self.buf.at[pl.ds(row * RING + self.low * i, RING - self.low if i else self.low)]

    def rows(self):
        for copy in self.b:
            copy.wait_recv()
        self.early, self.late = [], []
        for group, flip in ((self.early, 0), (self.late, 1)):
            for i, by in enumerate((1, -1)):
                ref = self.part(self.c2, i ^ flip)
                group.append(self.copy(ref, ref, 4 + 2 * flip + i, 1, by))
        self.to_sibling(self.buf.at[pl.ds(self.c2 * RING, RING)])

    def pass_rows(self):
        self.f = []
        for i, by in enumerate((1, -1)):
            self.early[i].wait_recv()
            ref = self.part(step(self.c2, -by), i)
            self.f.append(self.copy(ref, ref, 8 + i, 1, by))
            self.to_sibling(ref)

    def rest(self):
        for i, by in enumerate((1, -1)):
            self.late[i].wait_recv()
            self.to_sibling(self.part(step(self.c2, -by), 1 - i))

    def last(self):
        for i in range(2):
            self.f[i].wait_recv()
            self.to_sibling(self.part(step(self.c2, 2), i))

    def done(self):
        for copy in self.sib:
            copy.wait_recv()


def block_kernel(
    tok_ref, gain_ref, wq_ref, wk_ref, wv_ref, wo_ref, qg_ref, kg_ref, cos_ref, sin_ref,
    out_ref,
    tokbuf, wbuf, wo_bufs, xbuf, acc, sums, kvbuf, relay, heads, others, sbuf, rhalf, rfull,
    wsend, wrecv, sib_send, sib_recv, loc, tok_sem,
    ssend, srecv, xsend, xrecv, xssend, xsrecv, hsend, hrecv, osend, orecv, rsend, rrecv,
):
    x, y, z, r = place()
    width, rows = tok_ref.shape
    count = RING * RING
    seq = z * RING + x
    one = 1 - r

    def along1(by):
        return device(step(x, by * one), y, step(z, by * r), r)

    def along2(by):
        return device(step(x, by * r), y, step(z, by * one), r)

    def along_x(by):
        return device(step(x, by), y, z, r)

    def along_y(by):
        return device(x, step(y, by), z, r)

    def along_z(by):
        return device(x, y, step(z, by), r)

    def at_seq(s):
        return {"seq": s, "hid": y, "rep": r}

    def around(s):
        return lax.rem(s + count, count)

    sibling = device(x, y, z, 1 - r)
    after = at_seq(around(seq + 1))
    before = at_seq(around(seq - 1))
    via = device(step(x, -1), y, step(z, lax.div(x + 2, RING)), r)
    back = step(x, 1)
    via_from = device(back, y, step(z, -lax.div(back + 2, RING)), r)
    arrived = greet([along_x(1), along_x(-1), along_z(1), along_z(-1),
                     along_y(1), along_y(-1), along_y(2),
                     sibling, after, before, via, via_from])

    sent = []

    def go(*args):
        copy = send(*args)
        sent.append(copy)
        return copy

    def sems(ph):
        side = max(ph - 2, 0)
        return wsend.at[ph], wrecv.at[ph], sib_send.at[side], sib_recv.at[side], loc.at[ph]

    c1, c2 = x * one + z * r, z * one + x * r
    cols, depth = wbuf.shape[3], wbuf.shape[2]
    half = cols // 2

    def core_cols(size):
        return pl.ds(pl.multiple_of(r * size, size), size)

    tok = tokbuf
    fetch = pltpu.make_async_copy(tok_ref, tok, tok_sem)
    kv = Gather(go, [(wk_ref.at[:, core_cols(half)], 0, half), (wv_ref.at[:, core_cols(half)], half, half)],
                wbuf.at[0], c1, c2, along1, along2, None, sems(0))
    fetch.start()
    qq = Gather(go, [(wq_ref.at[:, core_cols(cols)], 0, cols)],
                wbuf.at[1], c1, c2, along1, along2, None, sems(1))
    qq.low = 1
    outs, starts = [], []
    for n, buf in enumerate(wo_bufs):
        starts.append(sum(b.shape[2] for b in wo_bufs[:n]))
        src = wo_ref.at[pl.ds(starts[n], buf.shape[2]), core_cols(cols)]
        outs.append(Gather(go, [(src, 0, cols)], buf.at[r], c1, c2, along1, along2, sibling,
                           sems(2 + n)))

    fetch.wait()
    raw = tok[...].astype(F32)
    sums[y] = jnp.sum(raw * raw, axis=0, keepdims=True)
    arrived()
    kv.start()
    told = [go(sums.at[y], sums.at[y], ssend.at[i], srecv.at[i], along_y(by))
            for i, by in enumerate((1, 2, 3))]
    for one_of in (qq, *outs):
        one_of.start()
    for one_of in (kv, qq, *outs):
        one_of.pass_first()
    for copy in told:
        copy.wait_recv()
    total = sums[0] + sums[1] + sums[2] + sums[3]
    scale = lax.rsqrt(total * (1.0 / (RING * width)) + 1e-06)

    lanes = 128
    chunk = rows // 2
    part_rows = chunk // 2

    skew = lax.rem(y * width, lanes)

    def rows_of(c):
        return pl.ds(c * chunk, chunk)

    def norm(c):
        mine = scale[:, c * chunk:(c + 1) * chunk]

        def norm_at(at, size):
            part = tok[pl.ds(at, size), rows_of(c)].astype(F32)
            wide = 2 * size if size == lanes else lanes
            seen = gain_ref[:, pl.ds(pl.multiple_of(y * width - skew + at, lanes), wide)]
            gain = jnp.where(skew == 0, seen[:, :size], seen[:, lanes // 2:lanes // 2 + size])
            xbuf[r, y, rows_of(c), pl.ds(at, size)] = ((part * mine).T * gain).astype(BF16)

        def norm_step(i, carry):
            norm_at(pl.multiple_of(i * lanes, lanes), lanes)
            return carry

        lax.fori_loop(0, width // lanes, norm_step, 0)
        if width % lanes:
            norm_at(width // lanes * lanes, width % lanes)

    def x_part(block, i):
        return xbuf.at[r, block, pl.ds(i * part_rows, part_rows)]

    x_early, x_late, x_last, x_sib = {}, {}, {}, {0: [], 1: []}

    def x_over(c, ref):
        i = 7 * c + len(x_sib[c])
        x_sib[c].append(go(ref, ref, xssend.at[i], xsrecv.at[i], sibling))

    def x_send(c):
        for flip, group in enumerate((x_early, x_late)):
            group[c] = []
            for i, by in enumerate((1, -1)):
                ref = x_part(y, 2 * c + (i ^ flip))
                at = 6 * c + 2 * flip + i
                group[c].append(go(ref, ref, xsend.at[at], xrecv.at[at], along_y(by)))
        x_over(c, xbuf.at[r, y, rows_of(c)])

    def x_pass(c):
        x_last[c] = []
        for i, by in enumerate((1, -1)):
            x_early[c][i].wait_recv()
            ref = x_part(step(y, -by), 2 * c + i)
            at = 6 * c + 4 + i
            x_last[c].append(go(ref, ref, xsend.at[at], xrecv.at[at], along_y(by)))
            x_over(c, ref)

    def x_rest(c):
        for i, by in enumerate((1, -1)):
            x_late[c][i].wait_recv()
            x_over(c, x_part(step(y, -by), 2 * c + 1 - i))

    def x_end(c):
        for i in range(2):
            x_last[c][i].wait_recv()
            x_over(c, x_part(step(y, 2), 2 * c + i))

    def slots(kind, t, j):
        low = 1 - kind
        return t * (RING * low + kind) + j * (low + RING * kind)

    def multiply(ph, h, at, first):
        right = jnp.concatenate([wbuf[ph, slots(r, h, j)] for j in range(RING)], axis=0)
        for side in range(2):
            part = jnp.dot(xbuf[side, h, at], right, preferred_element_type=F32)
            if first:
                acc[side, at] = part
            else:
                acc[side, at] += part

    def turn(u, gain, at):
        u = u * lax.rsqrt(jnp.mean(u * u, axis=-1, keepdims=True) + 1e-06) * gain
        cosine, sine = cos_ref[at], sin_ref[at]
        cosine = jnp.concatenate([cosine, cosine], axis=1)
        sine = jnp.concatenate([-sine, sine], axis=1)
        return u * cosine + pltpu.roll(u, HEAD_WIDTH // 2, 1) * sine

    key_gain, query_gain = kg_ref[...], qg_ref[...]
    pair_width = 2 * HEAD_WIDTH

    def block_rows(i, c):
        return pl.ds(i * rows + c * chunk, chunk)

    def keys_values(c):
        at = rows_of(c)

        def of_side(side, carry):
            for head in range(2):
                cols = pl.ds(head * HEAD_WIDTH, HEAD_WIDTH)
                kvbuf[side, block_rows(2, c), cols] = turn(acc[side, at, cols], key_gain, at).astype(BF16)
            cols = pl.ds(pair_width, pair_width)
            kvbuf[side, block_rows(2, c), cols] = acc[side, at, cols].astype(BF16)
            return carry

        lax.fori_loop(0, 2, of_side, 0)

    halo = {}

    def halo_go(c, i, src, dst, dev):
        halo[c, i] = go(src, dst, hsend.at[5 * c + i], hrecv.at[5 * c + i], dev)

    def halo_send(c):
        own0, own1 = (kvbuf.at[side, block_rows(2, c)] for side in range(2))
        halo_go(c, 0, own0, kvbuf.at[0, block_rows(1, c)], after)
        halo_go(c, 2, own1, relay.at[c], via)
        halo_go(c, 1, own1, kvbuf.at[1, block_rows(1, c)], after)

    def halo_pass(c):
        halo[c, 0].wait_recv()
        halo_go(c, 3, kvbuf.at[0, block_rows(1, c)], kvbuf.at[0, block_rows(0, c)], after)
        halo[c, 2].wait_recv()
        halo_go(c, 4, relay.at[c], kvbuf.at[1, block_rows(0, c)], along_x(-1))

    norm(1)
    x_send(1)
    kv.rows()
    norm(0)
    kv.pass_rows()
    qq.rows()
    x_pass(1)
    x_send(0)
    x_rest(1)
    kv.rest()
    x_end(1)
    kv.last()
    for copy in x_sib[1]:
        copy.wait_recv()
    multiply(0, y, rows_of(1), True)
    lax.fori_loop(1, RING, lambda i, c: (multiply(0, step(y, i), rows_of(1), False), c)[1], 0)
    keys_values(1)
    halo_send(1)
    x_pass(0)
    qq.pass_rows()
    x_rest(0)
    for copy in x_sib[0]:
        copy.wait_recv()
    multiply(0, y, rows_of(0), True)
    halo_pass(1)
    lax.fori_loop(0, 2, lambda i, c: (multiply(0, step(y, 1 + 2 * i), rows_of(0), False), c)[1], 0)
    x_end(0)
    for copy in x_sib[0][5:]:
        copy.wait_recv()
    multiply(0, step(y, 2), rows_of(0), False)
    keys_values(0)
    halo_send(0)
    qq.rest()
    qq.last()
    whole = pl.ds(0, rows)
    multiply(1, y, whole, True)
    lax.fori_loop(1, RING, lambda i, c: (multiply(1, step(y, i), whole, False), c)[1], 0)

    def queries(side, carry):
        for head in range(4):
            cols = pl.ds(head * HEAD_WIDTH, HEAD_WIDTH)
            turned = turn(acc[side, :, cols], query_gain, whole) * QSCALE ** (-0.5)
            heads[side, :, cols] = turned.astype(BF16)
        return carry

    lax.fori_loop(0, 2, queries, 0)
    halo_pass(0)
    outs[0].rows()
    for c in (1, 0):
        for i in (1, 3, 4):
            halo[c, i].wait_recv()

    span = WINDOW + QB
    ri = lax.broadcasted_iota(jnp.int32, (QB, QB), 0)
    ci = lax.broadcasted_iota(jnp.int32, (QB, QB), 1)
    recent = jnp.concatenate([ci <= ri] * 2, axis=0)
    oldest = jnp.concatenate([ci > ri] * 2, axis=0)
    lane = lax.broadcasted_iota(jnp.int32, (1, span), 1)

    def attend(side, it):
        g = lax.rem(it, 2)
        i = lax.div(it, 2)
        at = pl.multiple_of(i * QB, QB)
        k_cols = pl.ds(pl.multiple_of(g * HEAD_WIDTH, HEAD_WIDTH), HEAD_WIDTH)
        v_cols = pl.ds(pl.multiple_of((2 + g) * HEAD_WIDTH, HEAD_WIDTH), HEAD_WIDTH)
        pair = [pl.ds(pl.multiple_of((2 * g + j) * HEAD_WIDTH, HEAD_WIDTH), HEAD_WIDTH)
                for j in range(2)]
        q = jnp.concatenate([heads[side, pl.ds(at, QB), c] for c in pair], axis=0)
        k = kvbuf[side, pl.ds(at, span), k_cols]
        v = kvbuf[side, pl.ds(at, span), v_cols]
        s = lax.dot_general(q, k, (((1,), (1,)), ((), ())), preferred_element_type=F32)
        present = lane + at >= DEPTH * rows - seq * rows
        s = jnp.concatenate([
            jnp.where(oldest, s[:, :QB], -jnp.inf), s[:, QB:WINDOW],
            jnp.where(recent, s[:, WINDOW:], -jnp.inf)], axis=1)
        s = jnp.where(present, s, -jnp.inf)
        p = jnp.exp(s - jnp.max(s, axis=1, keepdims=True))
        p = (p * (1.0 / jnp.sum(p, axis=1, keepdims=True))).astype(BF16)
        o = jnp.dot(p, v, preferred_element_type=F32).astype(BF16)
        for j in range(2):
            heads[side, pl.ds(at, QB), pair[j]] = o[j * QB:(j + 1) * QB]

    def attend_all(side):
        lax.fori_loop(0, 2 * (rows // QB), lambda it, c: (attend(side, it), c)[1], 0)

    attend_all(1 - r)
    swap = go(heads.at[1 - r], others, osend, orecv, sibling)
    outs[0].pass_rows()
    outs[1].rows()
    attend_all(r)
    outs[0].rest()
    outs[0].last()
    swap.wait_recv()

    near, far = pl.ds(0, chunk), pl.ds(chunk, chunk)
    flows = {}

    def terms(n, t, dest):
        buf = wo_bufs[n]
        start, size = starts[n], buf.shape[2]

        def one_piece(j, carry):
            part = lax.dot_general(buf[r, slots(r, t, j)], heads[r], (((1,), (1,)), ((), ())),
                                   preferred_element_type=F32)
            part += lax.dot_general(buf[1 - r, slots(1 - r, t, j)], others[...],
                                    (((1,), (1,)), ((), ())), preferred_element_type=F32)
            dest[j, pl.ds(start, size), :] = part.astype(BF16)
            return carry

        lax.fori_loop(0, RING, one_piece, 0)

    def cut(n):
        return pl.ds(starts[n], wo_bufs[n].shape[2])

    def flow(n, i, src, dst, by):
        flows[n, i] = go(src, dst, rsend.at[6 * n + i], rrecv.at[6 * n + i], along_y(by))

    def spread(n):
        at = cut(n)
        terms(n, step(y, 2), sbuf.at[0])
        flow(n, 0, sbuf.at[0, :, at, near], rhalf.at[0, :, at], 1)
        flow(n, 1, sbuf.at[0, :, at, far], rhalf.at[1, :, at], -1)
        terms(n, step(y, 1), sbuf.at[1])
        flow(n, 2, sbuf.at[1, :, at, far], rfull.at[0, :, at, far], 1)
        terms(n, step(y, -1), sbuf.at[2])
        flow(n, 3, sbuf.at[2, :, at, near], rfull.at[1, :, at, near], -1)

    def add(n):
        at = cut(n)
        for i, half, by in ((0, near, 1), (1, far, -1)):
            flows[n, i].wait_recv()
            both = sbuf[1 + i, :, at, half].astype(F32) + rhalf[i, :, at].astype(F32)
            sbuf[1 + i, :, at, half] = both.astype(BF16)
            flow(n, 4 + i, sbuf.at[1 + i, :, at, half], rfull.at[i, :, at, half], by)

    def close(n):
        at = cut(n)
        for i in range(2, 6):
            flows[n, i].wait_recv()
        out_ref[:, at, :] = (out_ref[:, at, :].astype(F32) + rfull[0, :, at, :].astype(F32)
                             + rfull[1, :, at, :].astype(F32)).astype(BF16)

    for n in range(len(outs)):
        outs[n].done()
        spread(n)
        if n + 1 < len(outs):
            outs[n + 1].pass_rows()
        if n + 2 < len(outs):
            outs[n + 2].rows()
        terms(n, y, out_ref)
        add(n)
        if n + 1 < len(outs):
            outs[n + 1].rest()
            outs[n + 1].last()
    for n in range(len(outs)):
        close(n)
    for copy in sent:
        copy.wait_send()


def block(tok, gain, wq, wk, wv, wo, query_gain, key_gain, cosine, sine):
    width, rows = tok.shape
    depth, cols = wk.shape
    parts = len(OUT_PARTS)
    dma = pltpu.SemaphoreType.DMA
    vmem = pl.BlockSpec(memory_space=pltpu.VMEM)
    hbm = pl.BlockSpec(memory_space=pl.ANY)
    return pl.pallas_call(
        block_kernel,
        out_shape=jax.ShapeDtypeStruct((RING, depth, rows), BF16),
        in_specs=[hbm, vmem, hbm, hbm, hbm, hbm, vmem, vmem, vmem, vmem],
        out_specs=vmem,
        scratch_shapes=[
            pltpu.VMEM((width, rows), BF16),
            pltpu.VMEM((2, RING * RING, depth, cols), BF16),
            [pltpu.VMEM((2, RING * RING, size, cols), BF16) for size in OUT_PARTS],
            pltpu.VMEM((2, RING, rows, width), BF16),
            pltpu.VMEM((2, rows, cols), F32),
            pltpu.VMEM((RING, 1, rows), F32),
            pltpu.VMEM((2, 3 * rows, cols), BF16),
            pltpu.VMEM((2, rows // 2, cols), BF16),
            pltpu.VMEM((2, rows, cols), BF16),
            pltpu.VMEM((rows, cols), BF16),
            pltpu.VMEM((3, RING, depth, rows), BF16),
            pltpu.VMEM((2, RING, depth, rows // 2), BF16),
            pltpu.VMEM((2, RING, depth, rows), BF16),
            dma((2 + parts, 10)), dma((2 + parts, 10)), dma((parts, 7)), dma((parts, 7)),
            dma((2 + parts, 2)), dma,
            dma((3,)), dma((3,)), dma((12,)), dma((12,)), dma((14,)), dma((14,)),
            dma((10,)), dma((10,)), dma, dma, dma((6 * parts,)), dma((6 * parts,)),
        ],
        compiler_params=pltpu.CompilerParams(
            collective_id=0, has_side_effects=True, vmem_limit_bytes=VMEM_BYTES
        ),
    )(tok, gain, wq, wk, wv, wo, query_gain, key_gain, cosine, sine)


def shards(tokens, norm_gain, w_query, w_key, w_value, query_gain, key_gain, w_out):
    rows, width = tokens.shape
    base = lax.axis_index("seq") * rows
    qpos = base + jnp.arange(rows, dtype=jnp.int32)
    half = HEAD_WIDTH // 2
    freq = 10000.0 ** (-(jnp.arange(half, dtype=F32) * 2.0) / HEAD_WIDTH)
    angle = qpos.astype(F32)[:, None] * freq[None, :]
    cosine, sine = jnp.cos(angle), jnp.sin(angle)
    return block(
        tokens.T, norm_gain.reshape(1, -1), w_query, w_key, w_value, w_out.T,
        query_gain.reshape(1, -1), key_gain.reshape(1, -1), cosine, sine,
    ).reshape(width, rows).T


def solution(mesh):
    return jax.shard_map(
        shards,
        mesh=mesh,
        in_specs=(
            P(("rep", "seq"), "hid"),
            P(),
            P("seq", "hid"),
            P("seq", "hid"),
            P("seq", "hid"),
            P(),
            P(),
            P("hid", "seq"),
        ),
        out_specs=P(("rep", "seq"), "hid"),
        check_vma=False,
    )
```
